32 devices in a mesh: groups: 1, seq: 16 (over z, y, core), head: 2 (over x), dp: 1.
Axes of the slice: x: 2, y: 2, z: 4, core: 2. Of those that a mesh axis runs over, the one named last changes fastest.
Arguments:
- queries: bfloat16 [1, 4096, 1024], P(('groups', 'dp'), 'seq', 'head'), may hold values from -3 to 3
- keys_in: bfloat16 [1, 4096, 1024], P(('groups', 'dp'), 'seq', 'head'), may hold values from -3 to 3
- values: bfloat16 [1, 4096, 1024], P(('groups', 'dp'), 'seq', 'head'), may hold values from -6 to 6
- grad_out: bfloat16 [1, 4096, 1024], P(('groups', 'dp'), 'seq', 'head'), may hold values from -3 to 3
- latent: bfloat16 [1, 4096, 16], P(('groups', 'dp'), 'seq'), may hold values from -16 to 4
- gate_weight: bfloat16 [16, 8], P(None, 'head')
- gate_bias: float32 [8], P('head')
- doc_starts: int32 [1, 33], P(('groups', 'dp')), may hold values from 0 to 4096, as said below
- block_docs: int32 [1, 16], P(('groups', 'dp'), 'seq'), may hold values from 0 to 31, as said below
Outputs:
- grad_queries: bfloat16 [1, 4096, 1024], P(('groups', 'dp'), 'seq', 'head')
- grad_keys: bfloat16 [1, 4096, 1024], P(('groups', 'dp'), 'seq', 'head')
- grad_values: bfloat16 [1, 4096, 1024], P(('groups', 'dp'), 'seq', 'head')
- grad_latent: float32 [1, 4096, 16], P(('groups', 'dp'), 'seq')
- grad_gate_weight: float32 [16, 8], P('groups', 'head')
The draws below stay inside these ranges and needn't reach their ends.
Inputs may be any that keep to these rules, and one draw needn't show every extreme that they name: `doc_starts`: row s lists the first positions of the stream's 32 documents in increasing order, beginning with 0 and followed by 4096. Entry (s, m) is the document of stream s that holds position m * 256: doc_starts[s, e] <= m * 256 < doc_starts[s, e + 1] for e = block_docs[s, m].
All inputs are finite; a program needn't handle non-finite values.
Results may differ from the reference program's by a relative error of at most 0.0095.
Values sent between devices are 32-bit elements; how exact they have to be, the bound alone decides.
A program may use at most 64 MiB of HBM per device.

```python
import math
import jax
import jax.numpy as jnp
from jax import lax

HEAD_DIM = 128
RANK = 16
TOK_DEV = 256
HEAD_TOTAL = 8
PACKED_STREAMS = 1
BLOCKS = 16
STREAM_LENGTH = 4096
DOCS = 32


def doc_layout(key):

    def single_stream(stream_key):
        random_subkeys = jax.random.split(stream_key, 3)
        half_len = STREAM_LENGTH // 2
        anchor = jax.random.randint(random_subkeys[0], (), 0, STREAM_LENGTH - half_len + 1)
        crowd_at = jax.random.randint(random_subkeys[1], (), 0, STREAM_LENGTH - STREAM_LENGTH // 4 + 1)
        position_index = jnp.arange(1, STREAM_LENGTH, dtype=jnp.int32)
        random_noise = jax.random.randint(random_subkeys[2], (STREAM_LENGTH - 1,), 0, 1024)
        inside = (position_index > anchor) & (position_index < anchor + half_len)
        crowded = (position_index >= crowd_at) & (position_index < crowd_at + STREAM_LENGTH // 4)
        priority = random_noise + jnp.where(crowded, 0, 1024) + jnp.where(inside, 4096, 0)
        ranking = jnp.argsort(priority * STREAM_LENGTH + position_index)
        chosen = jnp.sort(position_index[ranking[:DOCS - 1]])
        bounds = jnp.concatenate([jnp.zeros((1,), jnp.int32), chosen, jnp.full((1,), STREAM_LENGTH, jnp.int32)])
        firsts = jnp.arange(BLOCKS, dtype=jnp.int32) * TOK_DEV
        doc_index = jnp.sum((bounds[None, 1:DOCS] <= firsts[:, None]).astype(jnp.int32), axis=1)
        return (bounds, doc_index)
    return jax.vmap(single_stream)(jax.random.split(jax.random.fold_in(key, 7), PACKED_STREAMS))


def draw_doc_starts(key, part):
    return doc_layout(key)[0]


def draw_block_docs(key, part):
    return doc_layout(key)[1]


def draw_latent(key, part):
    random_subkeys = jax.random.split(jax.random.fold_in(key, 11), 3)
    position_index = jnp.arange(STREAM_LENGTH, dtype=jnp.int32)
    growth = 1.0 + 2.0 * position_index.astype(jnp.float32) / STREAM_LENGTH
    random_noise = jnp.clip(0.5 * jax.random.normal(random_subkeys[0], (PACKED_STREAMS, STREAM_LENGTH, RANK)), -1.0, 1.0)
    random_noise = random_noise * growth[None, :, None]
    levels = jax.random.uniform(random_subkeys[1], (PACKED_STREAMS, BLOCKS), minval=-1.0, maxval=1.0)
    levels = jnp.repeat(levels, TOK_DEV, axis=1)
    spike_location = jax.random.randint(random_subkeys[2], (PACKED_STREAMS, 3), 0, STREAM_LENGTH)
    spike_values = jnp.any(position_index[None, :, None] == spike_location[:, None, :], axis=2)
    leading_column = jnp.where(spike_values, -16.0, random_noise[:, :, 0])
    second_col = levels + 0.3 * random_noise[:, :, 1]
    return jnp.concatenate([leading_column[:, :, None], second_col[:, :, None], random_noise[:, :, 2:]], axis=2).astype(jnp.bfloat16)


def draw_gate_weight(key, part):
    random_subkeys = jax.random.split(jax.random.fold_in(key, 17), 3)
    spike_row = jax.random.uniform(random_subkeys[0], (1, HEAD_TOTAL), minval=0.75, maxval=1.15)
    baseline_row = jax.random.uniform(random_subkeys[1], (1, HEAD_TOTAL), minval=0.5, maxval=1.0)
    remaining_rows = jnp.clip(0.3 * jax.random.normal(random_subkeys[2], (RANK - 2, HEAD_TOTAL)), -1.0, 1.0)
    return jnp.concatenate([spike_row, baseline_row, remaining_rows], axis=0).astype(jnp.bfloat16)


def draw_gate_bias(key, part):
    random_subkeys = jax.random.split(jax.random.fold_in(key, 13), 3)
    fast_share = 0.5
    fast_heads = jax.random.uniform(random_subkeys[0], (HEAD_TOTAL,)) < fast_share
    slow_bias = math.log(STREAM_LENGTH) - 1.5 + jax.random.uniform(random_subkeys[1], (HEAD_TOTAL,))
    fast_bias = jax.random.uniform(random_subkeys[2], (HEAD_TOTAL,), minval=0.3, maxval=1.2)
    return jnp.where(fast_heads, fast_bias, slow_bias)


def steps_of(rng, extent, cuts, low, top_value):
    factor_of = 1.0
    for position, shards_of in cuts:
        heights = jax.random.uniform(jax.random.fold_in(jax.random.fold_in(rng, 6), position), (shards_of,), jnp.float32, low / len(cuts), top_value / len(cuts))
        factor_of = factor_of * jnp.repeat(jnp.exp(heights), extent[position] // shards_of).reshape((-1,) + (1,) * (len(extent) - 1 - position))
    return factor_of


def normal_values(key, dims, width, bound, cuts=(), kind=jnp.bfloat16):
    gain = steps_of(key, dims, cuts, -0.22, 0.18) if cuts else 1.0
    values = jax.random.normal(key, dims, jnp.float32) * width * gain
    return jnp.minimum(jnp.maximum(values, -bound), bound).astype(kind)


def setup_inputs(seed: int = 0, part: int = 0) -> dict:
    splits = jax.random.split(jax.random.key(seed), 10)
    own_keys = jax.random.split(jax.random.fold_in(splits[9], part), 10)
    return {
        "queries": normal_values(own_keys[0], (PACKED_STREAMS, STREAM_LENGTH, HEAD_TOTAL * HEAD_DIM), 0.5, 3.0, ((1, 16), (2, 2))),
        "keys_in": normal_values(own_keys[1], (PACKED_STREAMS, STREAM_LENGTH, HEAD_TOTAL * HEAD_DIM), 0.5, 3.0, ((1, 16), (2, 2))),
        "values": normal_values(own_keys[2], (PACKED_STREAMS, STREAM_LENGTH, HEAD_TOTAL * HEAD_DIM), 1.0, 6.0, ((1, 16), (2, 2))),
        "grad_out": normal_values(own_keys[3], (PACKED_STREAMS, STREAM_LENGTH, HEAD_TOTAL * HEAD_DIM), 0.5, 3.0, ((1, 16), (2, 2))),
        "latent": draw_latent(jax.random.fold_in(jax.random.fold_in(splits[9], part), 71), part),
        "gate_weight": draw_gate_weight(jax.random.fold_in(splits[9], 71), part),
        "gate_bias": draw_gate_bias(jax.random.fold_in(splits[9], 71), part),
        "doc_starts": draw_doc_starts(jax.random.fold_in(jax.random.fold_in(splits[9], part), 71), part),
        "block_docs": draw_block_docs(jax.random.fold_in(jax.random.fold_in(splits[9], part), 71), part),
    }


precise = lax.Precision.HIGHEST

def head_loss(query_col, key_col, value_col, decay_col, start_col, grad_col):
    scaling = 1.0 / math.sqrt(HEAD_DIM)
    causal = jnp.tril(jnp.ones((TOK_DEV, TOK_DEV), dtype=bool))

    def advance(carried_state, pieces):
        query_blk, key_blk, value_blk, decay_blk, start_blk, grad_blk = pieces
        cumulative = jnp.cumsum(decay_blk)
        doc_group = jnp.cumsum(start_blk)
        same_doc = causal & (doc_group[:, None] == doc_group[None, :])
        spread = jnp.where(same_doc, cumulative[:, None] - cumulative[None, :], 0.0)
        weights = jnp.where(same_doc, jnp.exp(spread), 0.0)
        scores = jnp.dot(query_blk, key_blk.T, precision=precise) * scaling * weights
        carry_in = jnp.where(doc_group == 0.0, jnp.exp(cumulative), 0.0)
        result = jnp.dot(scores, value_blk, precision=precise)
        result = result + (carry_in * scaling)[:, None] * jnp.dot(query_blk, carried_state, precision=precise)
        carry_out = jnp.where(doc_group == doc_group[-1], jnp.exp(cumulative[-1] - cumulative), 0.0)
        through = jnp.where(doc_group[-1] == 0.0, jnp.exp(cumulative[-1]), 0.0)
        carried_state = through * carried_state + jnp.dot((key_blk * carry_out[:, None]).T, value_blk, precision=precise)
        return (carried_state, jnp.sum(result * grad_blk))

    def blocks(tensor):
        return tensor.reshape((STREAM_LENGTH // TOK_DEV, TOK_DEV) + tensor.shape[1:])
    initial = jnp.zeros((HEAD_DIM, HEAD_DIM), jnp.float32)
    final_state, totals = lax.scan(advance, initial, (blocks(query_col), blocks(key_col), blocks(value_col), blocks(decay_col), blocks(start_col), blocks(grad_col)))
    return jnp.sum(totals)

def reference(queries, keys_in, values, grad_out, latent, gate_weight, gate_bias, doc_starts, block_docs):
    stream_count = queries.shape[0]
    gate_pre = jnp.einsum('slr,rh->slh', latent.astype(jnp.float32), gate_weight.astype(jnp.float32), precision=precise) + gate_bias
    log_decay = jax.nn.log_sigmoid(gate_pre) / 16.0
    position_index = jnp.arange(STREAM_LENGTH, dtype=jnp.int32)
    matches = jnp.any(position_index[None, :, None] == doc_starts[:, None, :], axis=2)
    firsts = jnp.arange(BLOCKS, dtype=jnp.int32) * TOK_DEV
    opening = jnp.take_along_axis(doc_starts, block_docs.astype(jnp.int32), axis=1) == firsts[None, :]
    opening = jnp.repeat(opening, TOK_DEV, axis=1)
    starts = jnp.where((position_index % TOK_DEV == 0)[None, :], opening, matches).astype(jnp.float32)

    def heads_first(tensor):
        shaped = tensor.astype(jnp.float32).reshape(stream_count, STREAM_LENGTH, HEAD_TOTAL, HEAD_DIM)
        return jnp.moveaxis(shaped, 2, 1).reshape(stream_count * HEAD_TOTAL, STREAM_LENGTH, HEAD_DIM)
    decay_cols = jnp.moveaxis(log_decay, 2, 1).reshape(stream_count * HEAD_TOTAL, STREAM_LENGTH)
    start_cols = jnp.repeat(starts, HEAD_TOTAL, axis=0)
    gradient = jax.grad(head_loss, argnums=(0, 1, 2, 3))

    def per_head(pieces):
        return gradient(pieces[0], pieces[1], pieces[2], pieces[3], pieces[4], pieces[5])
    results = lax.map(per_head, (heads_first(queries), heads_first(keys_in), heads_first(values), decay_cols, start_cols, heads_first(grad_out)))

    def restore(tensor):
        shaped = tensor.reshape(stream_count, HEAD_TOTAL, STREAM_LENGTH, HEAD_DIM)
        return jnp.moveaxis(shaped, 1, 2).reshape(stream_count, STREAM_LENGTH, HEAD_TOTAL * HEAD_DIM).astype(jnp.bfloat16)
    grad_decay = jnp.moveaxis(results[3].reshape(stream_count, HEAD_TOTAL, STREAM_LENGTH), 1, 2)
    grad_gate = grad_decay * jax.nn.sigmoid(-gate_pre) / 16.0
    grad_latent = jnp.einsum('slh,rh->slr', grad_gate, gate_weight.astype(jnp.float32), precision=precise)
    grad_gate_weight = jnp.einsum('slr,slh->rh', latent.astype(jnp.float32), grad_gate, precision=precise)
    return (restore(results[0]), restore(results[1]), restore(results[2]), grad_latent, grad_gate_weight)
```

```python
import functools
import math

import jax
import jax.numpy as jnp
from jax import lax
from jax.experimental import pallas as pl
from jax.experimental.pallas import tpu as pltpu
from jax.sharding import PartitionSpec as P

HEAD_DIM = 128
LANES = 128
PAIR = 2
SIDE = 2

MESH = pl.DeviceIdType.MESH
precise = lax.Precision.HIGHEST
F32 = jnp.float32
BF16 = jnp.bfloat16


def dot(left, right, over, precision=None):
    return lax.dot_general(
        left, right, (((over[0],), (over[1],)), ((), ())),
        precision=precision, preferred_element_type=F32,
    )


def halves(tensor):
    upper = tensor.astype(BF16)
    return upper, (tensor - upper.astype(F32)).astype(BF16)


def kernel(
    sizes,
    q_ref, k_ref, v_ref, g_ref, latent_ref, weight_ref, bias_ref, bounds_ref,
    gq_ref, gk_ref, gv_ref, glat_ref, gw_ref,
    rows_ref, cols_ref, iq_ref, ik_ref, iv_ref,
    t_ref, part_ref, mate_ref, agg_ref, chain_out, chain_in, side_out, side_in, back_out, state_ref,
    lat_slots, gw_slots,
    t_send, t_recv, mate_send, mate_recv, chain_send, chain_recv, side_send, side_recv,
    back_send, back_recv, lat_send, lat_recv, gw_send, gw_recv,
):
    seq_count, dp_count, head_devices, heads = sizes
    rows = q_ref.shape[0]
    half = heads // PAIR
    layer = PAIR * SIDE
    depth = seq_count // layer
    scaling = 1.0 / math.sqrt(HEAD_DIM)
    me = lax.axis_index("seq")
    my_dp = lax.axis_index("dp")
    my_head = lax.axis_index("head")
    core = lax.rem(me, PAIR)
    side = lax.rem(lax.div(me, PAIR), SIDE)
    level = lax.div(me, layer)
    group = level * layer
    mate = group + side * PAIR + (1 - core)
    across = group + (1 - side) * PAIR + core
    members = seq_count * dp_count
    flat = me * dp_count + my_dp

    def member(index):
        return {"seq": lax.div(index, dp_count), "dp": lax.rem(index, dp_count)}

    barrier = pltpu.get_barrier_semaphore()
    for away in range(1, members):
        pl.semaphore_signal(
            barrier, inc=1, device_id=member(lax.rem(flat + away, members)), device_id_type=MESH
        )
    for away in range(1, head_devices):
        pl.semaphore_signal(
            barrier, inc=1, device_id={"head": lax.rem(my_head + away, head_devices)},
            device_id_type=MESH,
        )

    gate_rows = dot(weight_ref[...], latent_ref[...], (1, 0))
    eye = lax.broadcasted_iota(jnp.int32, (heads, heads), 0) == lax.broadcasted_iota(
        jnp.int32, (heads, heads), 1
    )
    bias = jnp.sum(jnp.where(eye, bias_ref[...], 0.0), axis=1, keepdims=True)
    gate_rows = gate_rows + bias
    log_decay = (jnp.minimum(gate_rows, 0.0) - jnp.log1p(jnp.exp(-jnp.abs(gate_rows)))) / 16.0
    row_id = lax.broadcasted_iota(jnp.int32, (rows, rows), 0)
    col_id = lax.broadcasted_iota(jnp.int32, (rows, rows), 1)
    upto = (row_id <= col_id).astype(F32)
    cumul = dot(log_decay, upto, (1, 0), precise)
    first_pos = me * rows
    bounds = bounds_ref[...]
    position = first_pos + lax.broadcasted_iota(jnp.int32, (rows, bounds.shape[1]), 0)
    opened = jnp.where((bounds >= first_pos) & (bounds <= position), 1.0, 0.0).astype(BF16)
    docs = dot(jnp.ones((8, bounds.shape[1]), BF16), opened, (1, 1))
    doc_row = docs[0:1]
    doc_last = doc_row[:, rows - 1:]
    ending = cumul[:, rows - 1:]
    carry_in = jnp.where(doc_row == 0.0, jnp.exp(cumul), 0.0) * scaling
    carry_out = jnp.where(doc_row == doc_last, jnp.exp(ending - cumul), 0.0)
    through = jnp.where(doc_last == 0.0, jnp.exp(ending), 0.0)
    rows_ref[...] = jnp.zeros_like(rows_ref)
    rows_ref[0:heads] = cumul
    rows_ref[heads:2 * heads] = carry_in
    rows_ref[2 * heads:3 * heads] = carry_out
    rows_ref[3 * heads:3 * heads + 8] = docs
    cols_ref[...] = rows_ref[...].T
    own_through = jnp.broadcast_to(through, (heads, LANES))
    t_ref[core + PAIR * side, 0:heads] = own_through

    def column(index):
        return cols_ref[:, index:index + 1]

    def head_lanes(index):
        return pl.ds(index * HEAD_DIM, HEAD_DIM)

    pl.semaphore_wait(barrier, members - 1 + head_devices - 1)

    place = core + PAIR * side
    t_copies = []
    for away in range(1, layer):
        peer = lax.rem(place + away, layer)
        t_copies.append(pltpu.make_async_remote_copy(
            src_ref=t_ref.at[place], dst_ref=t_ref.at[place],
            send_sem=t_send.at[away], recv_sem=t_recv.at[place],
            device_id={"seq": group + peer}, device_id_type=MESH,
        ))
        t_copies[-1].start()

    for head in range(heads):
        lanes = head_lanes(head)
        keys = k_ref[:, lanes].astype(F32) * column(2 * heads + head)
        upper, lower = halves(keys)
        value = v_ref[:, lanes]
        part_ref[0, head] = dot(upper, value, (0, 0)) + dot(lower, value, (0, 0))
        query = q_ref[:, lanes].astype(F32) * column(heads + head)
        upper, lower = halves(query)
        grad = g_ref[:, lanes]
        part_ref[1, head] = dot(upper, grad, (0, 0)) + dot(lower, grad, (0, 0))

    def mate_copy(way, j):
        return pltpu.make_async_remote_copy(
            src_ref=part_ref.at[way, (1 - core) * half + j], dst_ref=mate_ref.at[way, j],
            send_sem=mate_send.at[way, j], recv_sem=mate_recv.at[way, j],
            device_id={"seq": mate}, device_id_type=MESH,
        )

    for way in range(2):
        for j in range(half):
            mate_copy(way, j).start()

    for away in range(1, layer):
        source = lax.rem(place + layer - away, layer)
        pltpu.make_async_remote_copy(
            src_ref=t_ref.at[place], dst_ref=t_ref.at[source],
            send_sem=t_send.at[away], recv_sem=t_recv.at[source],
            device_id={"seq": group + source}, device_id_type=MESH,
        ).wait_recv()

    def decay_of(core_at, side_at, j):
        return t_ref[core_at + PAIR * side_at, pl.ds(core * half + j, 1), :]

    lower_mask = row_id >= col_id
    same_doc = lower_mask & (column(3 * heads) == doc_row)

    def local_head(head, sums):
        lanes = head_lanes(head)
        query, key, value, grad = q_ref[:, lanes], k_ref[:, lanes], v_ref[:, lanes], g_ref[:, lanes]
        spread = jnp.where(same_doc, column(head) - rows_ref[head:head + 1], 0.0)
        weights = jnp.where(same_doc, jnp.exp(spread), 0.0)
        scores = dot(query, key, (1, 1)) * scaling * weights
        pair_dots = dot(grad, value, (1, 1))
        weighted = (pair_dots * weights * scaling).astype(BF16)
        products = scores * pair_dots
        iv_ref[:, lanes] = dot(scores.astype(BF16), grad, (0, 0))
        iq_ref[:, lanes] = dot(weighted, key, (1, 0))
        ik_ref[:, lanes] = dot(weighted, query, (0, 0))
        sums.append(
            (jnp.sum(products, axis=1, keepdims=True), jnp.sum(products, axis=0, keepdims=True))
        )

    def chain_place(way):
        return jnp.where(way == 0, level, depth - 1 - level)

    def is_first(way, at):
        return jnp.where(way == 0, at, 1 - at) == 0

    def chain_copy(way, j):
        there = jnp.where(way == 0, level + 1, level - 1)
        return pltpu.make_async_remote_copy(
            src_ref=chain_out.at[way, j], dst_ref=chain_in.at[way, j],
            send_sem=chain_send.at[way, j], recv_sem=chain_recv.at[way, j],
            device_id={"seq": there * layer + side * PAIR + core}, device_id_type=MESH,
        )

    def side_copy(way, j):
        return pltpu.make_async_remote_copy(
            src_ref=side_out.at[way, j], dst_ref=side_in.at[way, j],
            send_sem=side_send.at[way, j], recv_sem=side_recv.at[way, j],
            device_id={"seq": across}, device_id_type=MESH,
        )

    def back_copy(way, j, owner):
        return pltpu.make_async_remote_copy(
            src_ref=back_out.at[way, j], dst_ref=state_ref.at[way, owner * half + j],
            send_sem=back_send.at[way, j], recv_sem=back_recv.at[way, j],
            device_id={"seq": mate}, device_id_type=MESH,
        )

    early = jnp.where(level * 2 < depth, 0, 1)

    def run_chain(way):
        here = chain_place(way)
        core_first = is_first(way, core)
        side_first = is_first(way, side)
        for j in range(half):
            mine, other = decay_of(core, side, j), decay_of(1 - core, side, j)
            chip = mine * other
            chip_other = decay_of(core, 1 - side, j) * decay_of(1 - core, 1 - side, j)
            mate_copy(way, j).wait_recv()
            agg_ref[way, j] = (
                jnp.where(core_first, other, 1.0) * part_ref[way, core * half + j]
                + jnp.where(core_first, 1.0, mine) * mate_ref[way, j]
            )

            @pl.when(here > 0)
            def _():
                chain_copy(way, j).wait_recv()

            @pl.when(here == 0)
            def _():
                chain_in[way, j] = jnp.zeros((HEAD_DIM, HEAD_DIM), F32)

            @pl.when(here < depth - 1)
            def _():
                chain_out[way, j] = (chip * chip_other) * chain_in[way, j] + jnp.where(
                    side_first, chip_other, 1.0
                ) * agg_ref[way, j]
                chain_copy(way, j).start()

            side_out[way, j] = jnp.where(side_first, chip, 1.0) * chain_in[way, j] + jnp.where(
                side_first, 1.0, 0.0
            ) * agg_ref[way, j]
            side_copy(way, j).start()

    def run_back(way):
        core_first = is_first(way, core)
        side_first = is_first(way, side)
        for j in range(half):
            mine, other = decay_of(core, side, j), decay_of(1 - core, side, j)
            chip_other = decay_of(core, 1 - side, j) * decay_of(1 - core, 1 - side, j)
            side_copy(way, j).wait_recv()
            entering = jnp.where(side_first, 1.0, chip_other) * chain_in[way, j] + side_in[way, j]
            back_out[way, j] = (
                jnp.where(core_first, mine, 1.0) * entering
                + jnp.where(core_first, 1.0, 0.0) * part_ref[way, core * half + j]
            )
            back_copy(way, j, core).start()
            state_ref[way, core * half + j] = (
                jnp.where(core_first, 1.0, other) * entering
                + jnp.where(core_first, 0.0, 1.0) * mate_ref[way, j]
            )

    sums = []
    run_chain(early)
    local_head(0, sums)
    if heads > 1:
        local_head(1, sums)
    run_chain(1 - early)
    for head in range(2, heads):
        local_head(head, sums)
    run_back(early)
    run_back(1 - early)
    for way in range(2):
        for j in range(half):
            back_copy(way, j, 1 - core).wait_recv()

    lane_id = lax.broadcasted_iota(jnp.int32, (rows, LANES), 1)
    gathered = jnp.zeros((rows, LANES), F32)
    ends = []
    for head in range(heads):
        lanes = head_lanes(head)
        query, key, value, grad = q_ref[:, lanes], k_ref[:, lanes], v_ref[:, lanes], g_ref[:, lanes]
        state, back = state_ref[0, head], state_ref[1, head]
        state_hi, state_lo = halves(state)
        back_hi, back_lo = halves(back)
        enter, leave = column(heads + head), column(2 * heads + head)
        grad_through = (dot(grad, state_hi, (1, 1)) + dot(grad, state_lo, (1, 1))) * enter
        key_carry = (dot(key, back_hi, (1, 0)) + dot(key, back_lo, (1, 0))) * leave
        value_carry = dot(value, back_hi, (1, 1)) * leave
        gq_ref[:, lanes] = (iq_ref[:, lanes] + grad_through).astype(BF16)
        gk_ref[:, lanes] = (ik_ref[:, lanes] + value_carry).astype(BF16)
        gv_ref[:, lanes] = (iv_ref[:, lanes] + key_carry).astype(BF16)
        inflow = jnp.sum(query.astype(F32) * grad_through, axis=1, keepdims=True)
        outflow = jnp.sum(value.astype(F32) * key_carry, axis=1, keepdims=True)
        whole = jnp.sum(jnp.sum(state * back, axis=0, keepdims=True), axis=1, keepdims=True)
        ends.append(
            through[head:head + 1] * whole + jnp.sum(outflow, axis=0, keepdims=True)
        )
        gathered = jnp.where(lane_id == head, sums[head][0] + inflow - outflow, gathered)
    turned = gathered.T[0:heads]
    across_sums = jnp.concatenate([s[1] for s in sums], axis=0)
    end_term = jnp.concatenate(ends, axis=0)
    row_lane = lax.broadcasted_iota(jnp.int32, (heads, rows), 1)
    grad_cumul = turned - across_sums + jnp.where(row_lane == rows - 1, end_term, 0.0)
    grad_log = dot(grad_cumul, (row_id >= col_id).astype(F32), (1, 0), precise)
    grad_gate = grad_log * (1.0 / (1.0 + jnp.exp(gate_rows))) / 16.0
    gw_part = dot(grad_gate, latent_ref[...].astype(F32), (1, 1), precise)
    gw_slots[flat, 0:heads, 0:gw_part.shape[1]] = gw_part
    lat_slots[my_head] = dot(weight_ref[...].astype(F32), grad_gate, (0, 0), precise)

    def lat_copy(away, slot, target):
        return pltpu.make_async_remote_copy(
            src_ref=lat_slots.at[slot], dst_ref=lat_slots.at[slot],
            send_sem=lat_send.at[away], recv_sem=lat_recv.at[slot],
            device_id={"head": target}, device_id_type=MESH,
        )

    def gw_copy(away, slot, target):
        return pltpu.make_async_remote_copy(
            src_ref=gw_slots.at[slot], dst_ref=gw_slots.at[slot],
            send_sem=gw_send.at[away], recv_sem=gw_recv.at[slot],
            device_id=member(target), device_id_type=MESH,
        )

    for away in range(1, members):
        gw_copy(away, flat, lax.rem(flat + away, members)).start()
    for away in range(1, head_devices):
        lat_copy(away, my_head, lax.rem(my_head + away, head_devices)).start()
    for away in range(1, head_devices):
        source = lax.rem(my_head + head_devices - away, head_devices)
        lat_copy(away, source, source).wait_recv()
    total = lat_slots[0]
    for slot in range(1, head_devices):
        total = total + lat_slots[slot]
    glat_ref[...] = total
    for away in range(1, members):
        source = lax.rem(flat + members - away, members)
        gw_copy(away, source, source).wait_recv()
    total = gw_slots[0]
    for slot in range(1, members):
        total = total + gw_slots[slot]
    gw_ref[...] = total

    for copy in t_copies:
        copy.wait_send()
    for way in range(2):
        for j in range(half):
            mate_copy(way, j).wait_send()
            side_copy(way, j).wait_send()
            back_copy(way, j, core).wait_send()

            @pl.when(chain_place(way) < depth - 1)
            def _():
                chain_copy(way, j).wait_send()
    for away in range(1, members):
        gw_copy(away, flat, lax.rem(flat + away, members)).wait_send()
    for away in range(1, head_devices):
        lat_copy(away, my_head, lax.rem(my_head + away, head_devices)).wait_send()


def final_kernel(gq, gk, gv, gl, gw, oq, ok, ov, ol, ow, sems):
    copies = []
    for i, (a, b) in enumerate(((gq, oq), (gk, ok), (gv, ov))):
        copies.append(pltpu.make_async_copy(a, b, sems.at[i]))
        copies[-1].start()
    ol[...] = gl[...]
    ow[...] = gw[0:ow.shape[0], 0:ow.shape[1]]
    for c in copies:
        c.wait()


def emit(out, rows, width, rank, heads):
    vm = pl.BlockSpec(memory_space=pltpu.VMEM)
    any_ = pl.BlockSpec(memory_space=pl.ANY)
    wide = jax.ShapeDtypeStruct((rows, width), BF16)
    return pl.pallas_call(
        final_kernel,
        out_shape=(wide, wide, wide, jax.ShapeDtypeStruct((rank, rows), F32), jax.ShapeDtypeStruct((heads, rank), F32)),
        in_specs=[vm] * 5,
        out_specs=(any_, any_, any_, vm, vm),
        scratch_shapes=[pltpu.SemaphoreType.DMA((3,))],
        name="emit",
    )(*(pltpu.with_memory_space_constraint(o, pltpu.VMEM) for o in out))


def on_device(sizes, *args):
    queries, keys_in, values, grad_out, latent, gate_weight, gate_bias, doc_starts, block_docs = args
    rows, width = queries.shape[1], queries.shape[2]
    rank = latent.shape[2]
    seq_count, dp_count, head_devices = sizes
    heads = width // HEAD_DIM
    half = heads // PAIR
    members = seq_count * dp_count
    depth = HEAD_DIM
    blocks = lambda *lead: pltpu.VMEM((*lead, depth, depth), F32)
    dma = lambda *shape: pltpu.SemaphoreType.DMA(shape)
    vmem = pl.BlockSpec(memory_space=pltpu.VMEM)
    wide = jax.ShapeDtypeStruct((rows, width), BF16)
    out = pl.pallas_call(
        functools.partial(kernel, (seq_count, dp_count, head_devices, heads)),
        out_shape=(
            pltpu.VMEM((rows, width), BF16), pltpu.VMEM((rows, width), BF16), pltpu.VMEM((rows, width), BF16),
            pltpu.VMEM((rank, rows), F32),
            pltpu.VMEM((8, LANES), F32),
        ),
        in_specs=[vmem] * 8,
        scratch_shapes=[
            pltpu.VMEM((LANES, rows), F32),
            pltpu.VMEM((rows, LANES), F32),
            pltpu.VMEM((rows, width), F32),
            pltpu.VMEM((rows, width), F32),
            pltpu.VMEM((rows, width), F32),
            pltpu.VMEM((PAIR * SIDE, 8, LANES), F32),
            blocks(2, heads), blocks(2, half), blocks(2, half), blocks(2, half), blocks(2, half),
            blocks(2, half), blocks(2, half), blocks(2, half), blocks(2, heads),
            pltpu.VMEM((head_devices, rank, rows), F32),
            pltpu.VMEM((members, 8, LANES), F32),
            dma(PAIR * SIDE), dma(PAIR * SIDE),
            dma(2, half), dma(2, half), dma(2, half), dma(2, half), dma(2, half), dma(2, half),
            dma(2, half), dma(2, half),
            dma(head_devices), dma(head_devices),
            dma(members), dma(members),
        ],
        compiler_params=pltpu.CompilerParams(collective_id=0, has_side_effects=True),
        name="gated_backward",
    )(
        queries[0], keys_in[0], values[0], grad_out[0], latent[0].T, gate_weight.T,
        gate_bias[None, :], doc_starts,
    )
    out = emit(out, rows, width, rank, heads)
    return (
        out[0][None], out[1][None], out[2][None], out[3].T[None], out[4].T,
    )


def solution(mesh):
    sizes = (mesh.shape["seq"], mesh.shape["dp"], mesh.shape["head"])
    return jax.shard_map(
        functools.partial(on_device, sizes),
        mesh=mesh,
        in_specs=(
            P(("groups", "dp"), "seq", "head"),
            P(("groups", "dp"), "seq", "head"),
            P(("groups", "dp"), "seq", "head"),
            P(("groups", "dp"), "seq", "head"),
            P(("groups", "dp"), "seq", None),
            P(None, "head"),
            P("head"),
            P(("groups", "dp"), None),
            P(("groups", "dp"), "seq"),
        ),
        out_specs=(
            P(("groups", "dp"), "seq", "head"),
            P(("groups", "dp"), "seq", "head"),
            P(("groups", "dp"), "seq", "head"),
            P(("groups", "dp"), "seq", None),
            P("groups", "head"),
        ),
        check_vma=False,
    )
```

```python
import functools
import math

import jax
import jax.numpy as jnp
from jax import lax
from jax.experimental import pallas as pl
from jax.experimental.pallas import tpu as pltpu
from jax.sharding import PartitionSpec as P

HEAD_DIM = 128
LANES = 128
PAIR = 2
CHIPS = 4
LEAD = 8
CHUNKS = 2
PIECE = HEAD_DIM // CHUNKS

MESH = pl.DeviceIdType.MESH
F32 = jnp.float32
BF16 = jnp.bfloat16


def dot(left, right, over):
    return lax.dot_general(
        left, right, (((over[0],), (over[1],)), ((), ())), preferred_element_type=F32,
    )


def halves(tensor):
    upper = tensor.astype(BF16)
    return upper, (tensor - upper.astype(F32)).astype(BF16)


def thirds(tensor):
    upper, rest = tensor.astype(BF16), None
    rest = tensor - upper.astype(F32)
    middle = rest.astype(BF16)
    return upper.astype(F32), middle.astype(F32), rest - middle.astype(F32)


def kernel(
    sizes,
    k_hbm, q_hbm, v_hbm, g_hbm, latent_hbm, weight_hbm, bias_hbm, bounds_hbm,
    gq_ref, gk_ref, gv_ref, glat_ref, gw_ref,
    x_ref, latent_ref, weight_ref, bias_ref, bounds_ref,
    stack_ref, rows_ref, cols_ref, upto_ref, iq_ref, ik_ref, iv_ref, flow_ref, down_ref,
    t_ref, part_ref, mate_in, rs_out, rs_in, blk_out, blk_in, ag_out, back_out, state_ref,
    lat_slots, gw_slots,
    load_sem, small_sem, t_send, t_recv, mate_send, mate_recv, rs_send, rs_recv,
    blk_send, blk_recv, ag_send, ag_recv, back_send, back_recv,
    lat_send, lat_recv, gw_send, gw_recv,
):
    seq_count, dp_count, head_devices, heads = sizes
    rows = x_ref.shape[1]
    quarter = heads // CHIPS
    layer = PAIR * CHIPS
    blocks = seq_count // layer
    pad = stack_ref.shape[0] // 3
    scaling = 1.0 / math.sqrt(HEAD_DIM)
    me = lax.axis_index("seq")
    my_dp = lax.axis_index("dp")
    my_head = lax.axis_index("head")
    core = lax.rem(me, PAIR)
    chip = lax.rem(lax.div(me, PAIR), CHIPS)
    block = lax.div(me, layer)
    group = block * layer
    place = core + PAIR * chip
    mate = me + 1 - 2 * core
    members = seq_count * dp_count
    flat = me * dp_count + my_dp
    beside = chip + 1 - 2 * lax.rem(chip, 2)
    above = chip + 2 - 4 * lax.div(chip, 2)
    opposite = CHIPS - 1 - chip
    others = (opposite, above, beside)

    def at_chip(index):
        return group + index * PAIR + core

    def at_block(distance):
        return me + jnp.where(core == 0, distance, -distance) * layer

    def sends_to(distance):
        return jnp.where(core == 0, block + distance < blocks, block >= distance)

    def hears_from(distance):
        return jnp.where(core == 0, block >= distance, block + distance < blocks)

    def member(index):
        return {"seq": lax.div(index, dp_count), "dp": lax.rem(index, dp_count)}

    small = [
        pltpu.make_async_copy(source, target, small_sem.at[index])
        for index, (source, target) in enumerate((
            (latent_hbm, latent_ref), (weight_hbm, weight_ref),
            (bias_hbm, bias_ref), (bounds_hbm, bounds_ref),
        ))
    ]
    loads = [
        pltpu.make_async_copy(source, x_ref.at[index], load_sem.at[index])
        for index, source in enumerate((k_hbm, q_hbm, v_hbm, g_hbm))
    ]
    for copy in small:
        copy.start()

    @pl.when(core == 0)
    def _():
        for index in (1, 3, 0, 2):
            loads[index].start()

    @pl.when(core == 1)
    def _():
        for index in (0, 2, 1, 3):
            loads[index].start()

    barrier = pltpu.get_barrier_semaphore()
    for away in range(1, members):
        pl.semaphore_signal(
            barrier, inc=1, device_id=member(lax.rem(flat + away, members)), device_id_type=MESH
        )
    for away in range(1, head_devices):
        pl.semaphore_signal(
            barrier, inc=1, device_id={"head": lax.rem(my_head + away, head_devices)},
            device_id_type=MESH,
        )

    row_id = lax.broadcasted_iota(jnp.int32, (rows, rows), 0)
    col_id = lax.broadcasted_iota(jnp.int32, (rows, rows), 1)
    upto_ref[...] = (row_id <= col_id).astype(F32).astype(BF16)
    stack_ref[...] = jnp.zeros_like(stack_ref)
    rows_ref[...] = jnp.zeros_like(rows_ref)
    flow_ref[...] = jnp.zeros_like(flow_ref)

    def stacked(tensor):
        for index, piece in enumerate(thirds(tensor)):
            stack_ref[index * pad:index * pad + heads] = piece
        return stack_ref[...].astype(BF16)

    def unstacked(tensor):
        return (tensor[0:heads] + tensor[pad:pad + heads]) + tensor[2 * pad:2 * pad + heads]

    for copy in small:
        copy.wait()
    gate_rows = dot(weight_ref[...], latent_ref[...], (1, 0))
    eye = lax.broadcasted_iota(jnp.int32, (heads, heads), 0) == lax.broadcasted_iota(
        jnp.int32, (heads, heads), 1
    )
    bias = jnp.sum(jnp.where(eye, bias_ref[...], 0.0), axis=1, keepdims=True)
    gate_rows = gate_rows + bias
    log_decay = (jnp.minimum(gate_rows, 0.0) - jnp.log1p(jnp.exp(-jnp.abs(gate_rows)))) / 16.0
    cumul = unstacked(dot(stacked(log_decay), upto_ref[...], (1, 0)))
    first_pos = me * rows
    bounds = bounds_ref[...]
    position = first_pos + lax.broadcasted_iota(jnp.int32, (rows, bounds.shape[1]), 0)
    opened = jnp.where((bounds >= first_pos) & (bounds <= position), 1.0, 0.0).astype(BF16)
    docs = dot(jnp.ones((8, bounds.shape[1]), BF16), opened, (1, 1))
    doc_row = docs[0:1]
    doc_last = doc_row[:, rows - 1:]
    ending = cumul[:, rows - 1:]
    through = jnp.where(doc_last == 0.0, jnp.exp(ending), 0.0)
    rows_ref[0:heads] = jnp.where(doc_row == doc_last, jnp.exp(ending - cumul), 0.0)
    rows_ref[heads:2 * heads] = jnp.where(doc_row == 0.0, jnp.exp(cumul), 0.0) * scaling
    rows_ref[2 * heads:3 * heads] = cumul
    rows_ref[3 * heads:3 * heads + 8] = docs
    t_ref[place, 0:heads] = jnp.broadcast_to(through, (heads, LANES))

    def column(index):
        return cols_ref[:, index:index + 1]

    def head_lanes(index):
        return pl.ds(index * HEAD_DIM, HEAD_DIM)

    def remote(source, target, send_sem, recv_sem, **where):
        return pltpu.make_async_remote_copy(
            src_ref=source, dst_ref=target, send_sem=send_sem, recv_sem=recv_sem,
            device_id=where, device_id_type=MESH,
        )

    pl.semaphore_wait(barrier, members - 1 + head_devices - 1)

    for away in range(1, layer):
        remote(
            t_ref.at[place], t_ref.at[place], t_send, t_recv,
            seq=group + lax.rem(place + away, layer),
        ).start()

    def mate_copy(head):
        return remote(
            part_ref.at[1 - core, head], mate_in.at[head], mate_send, mate_recv.at[head], seq=mate
        )

    def span(c):
        return pl.ds(c * PIECE, PIECE)

    def block_span(c):
        return pl.ds(0, LEAD + PIECE) if c == 0 else pl.ds(LEAD + c * PIECE, PIECE)

    def rs_copy(target, source, i, c):
        return remote(
            rs_out.at[target, i, span(c)], rs_in.at[source, i, span(c)],
            rs_send, rs_recv.at[source, c], seq=at_chip(target),
        )

    def blk_copy(distance, i, c):
        return remote(
            blk_out.at[i, block_span(c)], blk_in.at[distance - 1, i, block_span(c)],
            blk_send.at[distance - 1], blk_recv.at[distance - 1, c], seq=at_block(distance),
        )

    def ag_copy(target, source, i, c):
        return remote(
            ag_out.at[target, i, span(c)], state_ref.at[core, source * quarter + i, span(c)],
            ag_send, ag_recv.at[source, c], seq=at_chip(target),
        )

    def back_copy(head):
        return remote(
            back_out.at[head], state_ref.at[core, head], back_send, back_recv, seq=mate
        )

    order = [(whose, i) for whose in (*others, chip) for i in range(quarter)]

    def part(way, head):
        lanes = pl.ds(pl.multiple_of(head * HEAD_DIM, HEAD_DIM), HEAD_DIM)
        turned = x_ref[way, :, lanes].astype(F32).T
        upper, lower = halves(turned * rows_ref[pl.ds(way * heads + head, 1)])
        right = x_ref[2 + way, :, lanes]
        part_ref[way, head] = dot(upper, right, (1, 0)) + dot(lower, right, (1, 0))

    def load_wait(way):
        for index in (way, 2 + way):
            pltpu.make_async_copy(k_hbm, x_ref.at[index], load_sem.at[index]).wait()

    load_wait(1 - core)
    for whose, i in order:
        head = whose * quarter + i
        part(1 - core, head)
        mate_copy(head).start()
    load_wait(core)
    for whose, i in order:
        part(core, whose * quarter + i)

    passed = t_ref.at[pl.ds(0, layer - 1)]
    remote(passed, passed, t_send, t_recv, seq=mate).wait_recv()

    def decay_of(index, head):
        return t_ref[index, pl.ds(head, 1), :]

    for whose, i in order:
        head = whose * quarter + i
        keep = decay_of(PAIR * chip + 1 - core, head)
        mate_copy(head).wait_recv()
        for c in range(CHUNKS):
            total = keep * part_ref[core, head, span(c)] + mate_in[head, span(c)]
            if whose is chip:
                rs_in[chip, i, span(c)] = total
            else:
                rs_out[whose, i, span(c)] = total
                rs_copy(whose, chip, i, c).start()

    lane_id = lax.broadcasted_iota(jnp.int32, (rows, LANES), 1)

    def local_head(head):
        lanes = head_lanes(head)
        key, query, value, grad = (x_ref[index, :, lanes] for index in range(4))
        same_doc = (row_id >= col_id) & (column(3 * heads) == rows_ref[3 * heads:3 * heads + 1])
        spread = jnp.where(
            same_doc, column(2 * heads + head) - rows_ref[2 * heads + head:2 * heads + head + 1], 0.0
        )
        weights = jnp.where(same_doc, jnp.exp(spread), 0.0)
        scores = dot(query, key, (1, 1)) * scaling * weights
        pair_dots = dot(grad, value, (1, 1))
        weighted = (pair_dots * weights * scaling).astype(BF16)
        products = scores * pair_dots
        iv_ref[:, lanes] = dot(scores.astype(BF16), grad, (0, 0))
        iq_ref[:, lanes] = dot(weighted, key, (1, 0))
        ik_ref[:, lanes] = dot(weighted, query, (0, 0))
        flow_ref[...] += jnp.where(
            lane_id == head, jnp.sum(products, axis=1, keepdims=True), 0.0
        )
        down_ref[head:head + 1] = jnp.sum(products, axis=0, keepdims=True)

    cols_ref[...] = rows_ref[...].T
    for head in range(heads):
        local_head(head)

    def kth(k):
        return jnp.where(core == 0, k, CHIPS - 1 - k)

    def chip_decay(index, head):
        return decay_of(PAIR * index, head) * decay_of(PAIR * index + 1, head)

    for c in range(CHUNKS):
        for i in range(quarter):
            for source in others:
                rs_copy(source, source, i, c).wait_recv()
            head = chip * quarter + i
            total = rs_in[kth(0), i, span(c)]
            for k in range(1, CHIPS):
                total = chip_decay(kth(k), head) * total + rs_in[kth(k), i, span(c)]
            blk_out[i, pl.ds(LEAD + c * PIECE, PIECE)] = total
            if c == 0:
                across = chip_decay(0, head)
                for k in range(1, CHIPS):
                    across = across * chip_decay(k, head)
                blk_out[i, 0:LEAD] = jnp.broadcast_to(across, (LEAD, LANES))
            for distance in range(1, blocks):
                pl.when(sends_to(distance))(blk_copy(distance, i, c).start)

    for c in range(CHUNKS):
        for i in range(quarter):
            entering = jnp.zeros((PIECE, HEAD_DIM), F32)
            for distance in range(blocks - 1, 0, -1):
                hears = hears_from(distance)
                pl.when(hears)(blk_copy(distance, i, c).wait_recv)

                @pl.when(jnp.logical_not(hears))
                def _():
                    blk_in[distance - 1, i, block_span(c)] = jnp.zeros(
                        (PIECE + (LEAD if c == 0 else 0), HEAD_DIM), F32
                    )

                entering = (
                    blk_in[distance - 1, i, 0:1] * entering
                    + blk_in[distance - 1, i, pl.ds(LEAD + c * PIECE, PIECE)]
                )
            head = chip * quarter + i
            for k in range(CHIPS):
                ag_out[kth(k), i, span(c)] = entering
                if k < CHIPS - 1:
                    entering = chip_decay(kth(k), head) * entering + rs_in[kth(k), i, span(c)]
            for target in others:
                ag_copy(target, chip, i, c).start()

    for whose, i in ((whose, i) for whose in (chip, beside, above, opposite) for i in range(quarter)):
        head = whose * quarter + i
        if whose is chip:
            state_ref[core, head] = ag_out[chip, i]
        else:
            for c in range(CHUNKS):
                ag_copy(whose, whose, i, c).wait_recv()
        back_out[head] = decay_of(place, head) * state_ref[core, head] + part_ref[core, head]
        back_copy(head).start()

    def finish_state():
        for head in range(heads):
            lanes = head_lanes(head)
            query, grad = x_ref[1, :, lanes], x_ref[3, :, lanes]
            upper, lower = halves(state_ref[0, head])
            carried = (dot(grad, upper, (1, 1)) + dot(grad, lower, (1, 1))) * column(heads + head)
            gq_ref[:, lanes] = (iq_ref[:, lanes] + carried).astype(BF16)
            inflow = jnp.sum(query.astype(F32) * carried, axis=1, keepdims=True)
            flow_ref[...] += jnp.where(lane_id == head, inflow, 0.0)

    def finish_back():
        for head in range(heads):
            lanes = head_lanes(head)
            key, value = x_ref[0, :, lanes], x_ref[2, :, lanes]
            upper, lower = halves(state_ref[1, head])
            leave = column(head)
            carried = (dot(key, upper, (1, 0)) + dot(key, lower, (1, 0))) * leave
            gv_ref[:, lanes] = (iv_ref[:, lanes] + carried).astype(BF16)
            outflow = jnp.sum(value.astype(F32) * carried, axis=1, keepdims=True)
            flow_ref[...] -= jnp.where(lane_id == head, outflow, 0.0)
            total = jnp.sum(outflow, axis=0, keepdims=True)
            down_ref[heads + head:heads + head + 1] = jnp.broadcast_to(total, (1, rows))
            gk_ref[:, lanes] = (
                ik_ref[:, lanes] + dot(value, upper, (1, 1)) * leave
            ).astype(BF16)

    pl.when(core == 0)(finish_state)
    pl.when(core == 1)(finish_back)
    remote(back_out, state_ref.at[1 - core], back_send, back_recv, seq=mate).wait_recv()
    pl.when(core == 0)(finish_back)
    pl.when(core == 1)(finish_state)

    turned = flow_ref[...].T[0:heads]
    wholes = [
        jnp.sum(jnp.sum(state_ref[0, head] * state_ref[1, head], axis=0, keepdims=True), axis=1, keepdims=True)
        for head in range(heads)
    ]
    end_term = through * jnp.concatenate(wholes, axis=0) + down_ref[heads:2 * heads]
    row_lane = lax.broadcasted_iota(jnp.int32, (heads, rows), 1)
    grad_cumul = turned - down_ref[0:heads] + jnp.where(row_lane == rows - 1, end_term, 0.0)
    grad_log = unstacked(dot(stacked(grad_cumul), upto_ref[...], (1, 1)))
    grad_gate = grad_log * (1.0 / (1.0 + jnp.exp(gate_rows))) / 16.0
    pieces = stacked(grad_gate)
    gw_part = unstacked(dot(pieces, latent_ref[...], (1, 1)))
    gw_slots[flat, 0:heads, 0:gw_part.shape[1]] = gw_part
    weight = weight_ref[...]
    lat_slots[my_head] = (
        dot(weight, pieces[0:heads], (0, 0)) + dot(weight, pieces[pad:pad + heads], (0, 0))
    ) + dot(weight, pieces[2 * pad:2 * pad + heads], (0, 0))

    for away in range(1, members):
        remote(
            gw_slots.at[flat], gw_slots.at[flat], gw_send, gw_recv,
            **member(lax.rem(flat + away, members)),
        ).start()
    for away in range(1, head_devices):
        remote(
            lat_slots.at[my_head], lat_slots.at[my_head], lat_send, lat_recv,
            head=lax.rem(my_head + away, head_devices),
        ).start()

    peer = {"head": lax.rem(my_head + 1, head_devices)}
    if head_devices > 1:
        passed = lat_slots.at[pl.ds(0, head_devices - 1)]
        lats = remote(passed, passed, lat_send, lat_recv, **peer)
        lats.wait_recv()
    total = lat_slots[0]
    for slot in range(1, head_devices):
        total = total + lat_slots[slot]
    glat_ref[...] = total
    passed = gw_slots.at[pl.ds(0, members - 1)]
    sums = remote(passed, passed, gw_send, gw_recv, seq=mate)
    sums.wait_recv()
    total = gw_slots[0]
    for slot in range(1, members):
        total = total + gw_slots[slot]
    gw_ref[...] = total

    passed = t_ref.at[pl.ds(0, layer - 1)]
    remote(passed, passed, t_send, t_recv, seq=mate).wait_send()
    remote(mate_in, mate_in, mate_send, mate_recv.at[0], seq=mate).wait_send()
    passed = rs_out.at[pl.ds(0, CHIPS - 1)]
    remote(passed, passed, rs_send, rs_recv.at[0, 0], seq=mate).wait_send()
    passed = ag_out.at[pl.ds(0, CHIPS - 1)]
    remote(passed, passed, ag_send, ag_recv.at[0, 0], seq=mate).wait_send()
    remote(back_out, back_out, back_send, back_recv, seq=mate).wait_send()
    for distance in range(1, blocks):
        pl.when(sends_to(distance))(
            remote(
                blk_out, blk_out, blk_send.at[distance - 1], blk_recv.at[0, 0], seq=mate
            ).wait_send
        )
    if head_devices > 1:
        lats.wait_send()
    sums.wait_send()


def emit_kernel(gq, gk, gv, glat, gw, oq, ok, ov, olat, ow, sems):
    copies = [
        pltpu.make_async_copy(source, target, sems.at[index])
        for index, (source, target) in enumerate(((gq, oq), (gk, ok), (gv, ov)))
    ]
    for copy in copies:
        copy.start()
    olat[...] = glat[...]
    ow[...] = gw[0:ow.shape[0], 0:ow.shape[1]]
    for copy in copies:
        copy.wait()


def emit(results, rows, width, rank, heads):
    vmem = pl.BlockSpec(memory_space=pltpu.VMEM)
    hbm = pl.BlockSpec(memory_space=pl.ANY)
    wide = jax.ShapeDtypeStruct((rows, width), BF16)
    return pl.pallas_call(
        emit_kernel,
        out_shape=(
            wide, wide, wide,
            jax.ShapeDtypeStruct((rank, rows), F32), jax.ShapeDtypeStruct((heads, rank), F32),
        ),
        in_specs=[vmem] * 5,
        out_specs=(hbm, hbm, hbm, vmem, vmem),
        scratch_shapes=[pltpu.SemaphoreType.DMA((3,))],
        name="emit",
    )(*(pltpu.with_memory_space_constraint(result, pltpu.VMEM) for result in results))


def on_device(sizes, *args):
    queries, keys_in, values, grad_out, latent, gate_weight, gate_bias, doc_starts, block_docs = args
    rows, width = queries.shape[1], queries.shape[2]
    rank = latent.shape[2]
    seq_count, dp_count, head_devices = sizes
    heads = width // HEAD_DIM
    quarter = heads // CHIPS
    layer = PAIR * CHIPS
    far = max(1, seq_count // layer - 1)
    members = seq_count * dp_count
    pad = -(-heads // 8) * 8
    square = lambda *lead: pltpu.VMEM((*lead, HEAD_DIM, HEAD_DIM), F32)
    dma = lambda *shape: pltpu.SemaphoreType.DMA(shape)
    single = pltpu.SemaphoreType.DMA
    hbm = pl.BlockSpec(memory_space=pltpu.HBM)
    wide = pltpu.VMEM((rows, width), BF16)
    results = pl.pallas_call(
        functools.partial(kernel, (seq_count, dp_count, head_devices, heads)),
        out_shape=(
            wide, wide, wide, pltpu.VMEM((rank, rows), F32), pltpu.VMEM((8, LANES), F32),
        ),
        in_specs=[hbm] * 8,
        scratch_shapes=[
            pltpu.VMEM((4, rows, width), BF16),
            pltpu.VMEM((rank, rows), BF16),
            pltpu.VMEM((heads, rank), BF16),
            pltpu.VMEM((1, heads), F32),
            pltpu.VMEM(doc_starts.shape, jnp.int32),
            pltpu.VMEM((3 * pad, rows), F32),
            pltpu.VMEM((LANES, rows), F32),
            pltpu.VMEM((rows, LANES), F32),
            pltpu.VMEM((rows, rows), BF16),
            pltpu.VMEM((rows, width), F32),
            pltpu.VMEM((rows, width), F32),
            pltpu.VMEM((rows, width), F32),
            pltpu.VMEM((rows, LANES), F32),
            pltpu.VMEM((2 * pad, rows), F32),
            pltpu.VMEM((layer, 8, LANES), F32),
            square(2, heads), square(heads), square(CHIPS, quarter), square(CHIPS, quarter),
            pltpu.VMEM((quarter, LEAD + HEAD_DIM, HEAD_DIM), F32),
            pltpu.VMEM((far, quarter, LEAD + HEAD_DIM, HEAD_DIM), F32),
            square(CHIPS, quarter), square(heads), square(2, heads),
            pltpu.VMEM((head_devices, rank, rows), F32),
            pltpu.VMEM((members, 8, LANES), F32),
            dma(4), dma(4), single, single, single, dma(heads), single, dma(CHIPS, CHUNKS),
            dma(far), dma(far, CHUNKS), single, dma(CHIPS, CHUNKS), single, single,
            single, single, single, single,
        ],
        compiler_params=pltpu.CompilerParams(collective_id=0, has_side_effects=True),
        name="gated_backward",
    )(
        keys_in[0], queries[0], values[0], grad_out[0], latent[0].T, gate_weight.T,
        gate_bias[None, :], doc_starts,
    )
    out = emit(results, rows, width, rank, heads)
    return out[0][None], out[1][None], out[2][None], out[3].T[None], out[4].T


def solution(mesh):
    sizes = (mesh.shape["seq"], mesh.shape["dp"], mesh.shape["head"])
    return jax.shard_map(
        functools.partial(on_device, sizes),
        mesh=mesh,
        in_specs=(
            P(("groups", "dp"), "seq", "head"),
            P(("groups", "dp"), "seq", "head"),
            P(("groups", "dp"), "seq", "head"),
            P(("groups", "dp"), "seq", "head"),
            P(("groups", "dp"), "seq", None),
            P(None, "head"),
            P("head"),
            P(("groups", "dp"), None),
            P(("groups", "dp"), "seq"),
        ),
        out_specs=(
            P(("groups", "dp"), "seq", "head"),
            P(("groups", "dp"), "seq", "head"),
            P(("groups", "dp"), "seq", "head"),
            P(("groups", "dp"), "seq", None),
            P("groups", "head"),
        ),
        check_vma=False,
    )
```

```python
import functools
import math

import jax
import jax.numpy as jnp
from jax import lax
from jax.experimental import pallas as pl
from jax.experimental.pallas import tpu as pltpu
from jax.sharding import PartitionSpec as P

HEAD_DIM = 128
LANES = 128
PAIR = 2
CHIPS = 4
LEAD = 8
CHUNKS = 4
PIECE = HEAD_DIM // CHUNKS

MESH = pl.DeviceIdType.MESH
F32 = jnp.float32
BF16 = jnp.bfloat16


def dot(left, right, over):
    return lax.dot_general(
        left, right, (((over[0],), (over[1],)), ((), ())), preferred_element_type=F32,
    )


def halves(tensor):
    upper = tensor.astype(BF16)
    return upper, (tensor - upper.astype(F32)).astype(BF16)


def thirds(tensor):
    upper, rest = tensor.astype(BF16), None
    rest = tensor - upper.astype(F32)
    middle = rest.astype(BF16)
    return upper.astype(F32), middle.astype(F32), rest - middle.astype(F32)


def kernel(
    sizes,
    k_hbm, q_hbm, v_hbm, g_hbm, latent_hbm, weight_hbm, bias_hbm, bounds_hbm,
    gq_ref, gk_ref, gv_ref, glat_ref, gw_ref,
    x_ref, latent_ref, weight_ref, bias_ref, bounds_ref,
    tiled_ref, stack_ref, rows_ref, cols_ref, upto_ref, iq_ref, ik_ref, iv_ref, flow_ref, down_ref,
    t_ref, part_ref, mate_in, rs_out, rs_in, blk_out, blk_in, ag_out, back_out, state_ref,
    lat_slots, gw_slots,
    load_sem, small_sem, t_send, t_recv, mate_send, mate_recv, rs_send, rs_recv,
    blk_send, blk_recv, ag_send, ag_recv, back_send, back_recv,
    lat_send, lat_recv, gw_send, gw_recv, block_ready, head_ready,
):
    seq_count, dp_count, head_devices, heads = sizes
    rows = x_ref.shape[1]
    quarter = heads // CHIPS
    layer = PAIR * CHIPS
    blocks = seq_count // layer
    rank = latent_ref.shape[0]
    pad = stack_ref.shape[0] // 3
    scaling = 1.0 / math.sqrt(HEAD_DIM)
    me = lax.axis_index("seq")
    my_dp = lax.axis_index("dp")
    my_head = lax.axis_index("head")
    core = lax.rem(me, PAIR)
    chip = lax.rem(lax.div(me, PAIR), CHIPS)
    block = lax.div(me, layer)
    group = block * layer
    place = core + PAIR * chip
    mate = me + 1 - 2 * core
    members = seq_count * dp_count
    flat = me * dp_count + my_dp
    beside = chip + 1 - 2 * lax.rem(chip, 2)
    above = chip + 2 - 4 * lax.div(chip, 2)
    opposite = CHIPS - 1 - chip
    others = (opposite, above, beside)

    def at_chip(index):
        return group + index * PAIR + core

    def at_block(distance):
        return me + jnp.where(core == 0, distance, -distance) * layer

    def sends_to(distance):
        return jnp.where(core == 0, block + distance < blocks, block >= distance)

    def hears_from(distance):
        return jnp.where(core == 0, block >= distance, block + distance < blocks)

    def member(index):
        return {"seq": lax.div(index, dp_count), "dp": lax.rem(index, dp_count)}

    def greet(semaphore, **where):
        pl.semaphore_signal(semaphore, inc=1, device_id=where, device_id_type=MESH)

    small = [
        pltpu.make_async_copy(source, target, small_sem.at[index])
        for index, (source, target) in enumerate((
            (latent_hbm, latent_ref), (weight_hbm, weight_ref),
            (bias_hbm, bias_ref), (bounds_hbm, bounds_ref),
        ))
    ]
    loads = [
        pltpu.make_async_copy(source, x_ref.at[index], load_sem.at[index])
        for index, source in enumerate((k_hbm, q_hbm, v_hbm, g_hbm))
    ]
    for copy in small:
        copy.start()

    @pl.when(core == 0)
    def _():
        for index in (1, 3, 0, 2):
            loads[index].start()

    @pl.when(core == 1)
    def _():
        for index in (0, 2, 1, 3):
            loads[index].start()

    barrier = pltpu.get_barrier_semaphore()
    greeted = layer - 1 + seq_count * (dp_count - 1)
    for away in range(1, layer):
        greet(barrier, seq=group + lax.rem(place + away, layer))
    for away in range(1, dp_count):
        for there in range(seq_count):
            greet(barrier, seq=there, dp=lax.rem(my_dp + away, dp_count))
    for distance in range(1, blocks):

        @pl.when(block + distance < blocks)
        def _():
            greet(barrier, seq=me + distance * layer)

        greeted = greeted + jnp.where(block >= distance, 1, 0)
    for distance in range(1, head_devices):

        @pl.when(my_head + distance < head_devices)
        def _():
            greet(barrier, head=my_head + distance)

        greeted = greeted + jnp.where(my_head >= distance, 1, 0)

    row_id = lax.broadcasted_iota(jnp.int32, (rows, rows), 0)
    col_id = lax.broadcasted_iota(jnp.int32, (rows, rows), 1)
    upto_ref[...] = (row_id <= col_id).astype(F32).astype(BF16)
    stack_ref[...] = jnp.zeros_like(stack_ref)
    rows_ref[...] = jnp.zeros_like(rows_ref)
    flow_ref[...] = jnp.zeros_like(flow_ref)

    def stacked(tensor):
        for index, piece in enumerate(thirds(tensor)):
            stack_ref[index * pad:index * pad + heads] = piece
        return stack_ref[...].astype(BF16)

    def unstacked(tensor):
        return (tensor[0:heads] + tensor[pad:pad + heads]) + tensor[2 * pad:2 * pad + heads]

    for copy in small:
        copy.wait()
    gate_rows = dot(weight_ref[...], latent_ref[...], (1, 0))
    eye = lax.broadcasted_iota(jnp.int32, (heads, heads), 0) == lax.broadcasted_iota(
        jnp.int32, (heads, heads), 1
    )
    bias = jnp.sum(jnp.where(eye, bias_ref[...], 0.0), axis=1, keepdims=True)
    gate_rows = gate_rows + bias
    log_decay = (jnp.minimum(gate_rows, 0.0) - jnp.log1p(jnp.exp(-jnp.abs(gate_rows)))) / 16.0
    cumul = unstacked(dot(stacked(log_decay), upto_ref[...], (1, 0)))
    first_pos = me * rows
    bounds = bounds_ref[...]
    position = first_pos + lax.broadcasted_iota(jnp.int32, (rows, bounds.shape[1]), 0)
    opened = jnp.where((bounds >= first_pos) & (bounds <= position), 1.0, 0.0).astype(BF16)
    docs = dot(jnp.ones((8, bounds.shape[1]), BF16), opened, (1, 1))
    doc_row = docs[0:1]
    doc_last = doc_row[:, rows - 1:]
    ending = cumul[:, rows - 1:]
    through = jnp.where(doc_last == 0.0, jnp.exp(ending), 0.0)
    rows_ref[0:heads] = jnp.where(doc_row == doc_last, jnp.exp(ending - cumul), 0.0)
    rows_ref[heads:2 * heads] = jnp.where(doc_row == 0.0, jnp.exp(cumul), 0.0) * scaling
    rows_ref[2 * heads:3 * heads] = cumul
    rows_ref[3 * heads:3 * heads + 8] = docs
    t_ref[place, 0:heads] = jnp.broadcast_to(through, (heads, LANES))

    def column(index):
        return cols_ref[:, index:index + 1]

    def head_lanes(index):
        return pl.ds(index * HEAD_DIM, HEAD_DIM)

    def remote(source, target, send_sem, recv_sem, **where):
        return pltpu.make_async_remote_copy(
            src_ref=source, dst_ref=target, send_sem=send_sem, recv_sem=recv_sem,
            device_id=where, device_id_type=MESH,
        )

    pl.semaphore_wait(barrier, greeted)
    for distance in range(1, blocks):

        @pl.when(block >= distance)
        def _():
            greet(block_ready.at[distance - 1], seq=me - distance * layer)

    for distance in range(1, head_devices):

        @pl.when(my_head >= distance)
        def _():
            greet(head_ready.at[distance - 1], head=my_head - distance)


    def decay_copy(target, slot):
        return remote(
            t_ref.at[slot], t_ref.at[slot], t_send,
            t_recv.at[0 if target is mate else 1], seq=target,
        )

    decay_copy(mate, place).start()
    for whose in others:
        for peer in range(PAIR):
            decay_copy(group + whose * PAIR + peer, place).start()

    def mate_copy(head):
        return remote(
            part_ref.at[1 - core, head], mate_in.at[head], mate_send, mate_recv.at[head], seq=mate
        )

    def span(c):
        return pl.ds(c * PIECE, PIECE)

    def block_span(c):
        return pl.ds(0, LEAD + PIECE) if c == 0 else pl.ds(LEAD + c * PIECE, PIECE)

    def rs_copy(target, source, i, c):
        return remote(
            rs_out.at[target, i, span(c)], rs_in.at[source, i, span(c)],
            rs_send, rs_recv.at[source, c], seq=at_chip(target),
        )

    def blk_copy(distance, i, c):
        return remote(
            blk_out.at[i, block_span(c)], blk_in.at[distance - 1, i, block_span(c)],
            blk_send.at[distance - 1], blk_recv.at[distance - 1, c], seq=at_block(distance),
        )

    def ag_copy(target, source, i, c):
        return remote(
            ag_out.at[target, i, span(c)], state_ref.at[core, source * quarter + i, span(c)],
            ag_send, ag_recv.at[source, c], seq=at_chip(target),
        )

    def back_copy(head):
        return remote(
            back_out.at[head], state_ref.at[core, head], back_send, back_recv, seq=mate
        )

    order = [(whose, i) for whose in (*others, chip) for i in range(quarter)]

    def part(way, head):
        lanes = pl.ds(pl.multiple_of(head * HEAD_DIM, HEAD_DIM), HEAD_DIM)
        turned = x_ref[way, :, lanes].astype(F32).T
        upper, lower = halves(turned * rows_ref[pl.ds(way * heads + head, 1)])
        right = x_ref[2 + way, :, lanes]
        part_ref[way, head] = dot(upper, right, (1, 0)) + dot(lower, right, (1, 0))

    def load_wait(way):
        for index in (way, 2 + way):
            pltpu.make_async_copy(k_hbm, x_ref.at[index], load_sem.at[index]).wait()

    load_wait(1 - core)
    for whose, i in order:
        head = whose * quarter + i
        part(1 - core, head)
        mate_copy(head).start()
    load_wait(core)
    for whose, i in order:
        part(core, whose * quarter + i)

    decay_copy(mate, place).wait_recv()

    def decay_of(index, head):
        return t_ref[index, pl.ds(head, 1), :]

    for whose, i in order:
        head = whose * quarter + i
        keep = decay_of(PAIR * chip + 1 - core, head)
        mate_copy(head).wait_recv()
        for c in range(CHUNKS):
            total = keep * part_ref[core, head, span(c)] + mate_in[head, span(c)]
            if whose is chip:
                rs_in[chip, i, span(c)] = total
            else:
                rs_out[whose, i, span(c)] = total
                rs_copy(whose, chip, i, c).start()

    lane_id = lax.broadcasted_iota(jnp.int32, (rows, LANES), 1)

    def local_head(head):
        lanes = head_lanes(head)
        key, query, value, grad = (x_ref[index, :, lanes] for index in range(4))
        same_doc = (row_id >= col_id) & (column(3 * heads) == rows_ref[3 * heads:3 * heads + 1])
        spread = jnp.where(
            same_doc, column(2 * heads + head) - rows_ref[2 * heads + head:2 * heads + head + 1], 0.0
        )
        weights = jnp.where(same_doc, jnp.exp(spread), 0.0)
        scores = dot(query, key, (1, 1)) * scaling * weights
        pair_dots = dot(grad, value, (1, 1))
        weighted = (pair_dots * weights * scaling).astype(BF16)
        products = scores * pair_dots
        iv_ref[:, lanes] = dot(scores.astype(BF16), grad, (0, 0))
        iq_ref[:, lanes] = dot(weighted, key, (1, 0))
        ik_ref[:, lanes] = dot(weighted, query, (0, 0))
        flow_ref[...] += jnp.where(
            lane_id == head, jnp.sum(products, axis=1, keepdims=True), 0.0
        )
        down_ref[head:head + 1] = jnp.sum(products, axis=0, keepdims=True)

    for index in range(LANES // rank):
        tiled_ref[index * rank:(index + 1) * rank] = latent_ref[...]
    cols_ref[...] = rows_ref[...].T
    for head in range(heads):
        local_head(head)

    def kth(k):
        return jnp.where(core == 0, k, CHIPS - 1 - k)

    def chip_decay(index, head):
        return decay_of(PAIR * index, head) * decay_of(PAIR * index + 1, head)

    passed = t_ref.at[pl.ds(0, layer - PAIR)]
    remote(passed, passed, t_send, t_recv.at[1], seq=mate).wait_recv()
    for distance in range(1, blocks):

        @pl.when(block + distance < blocks)
        def _():
            pl.semaphore_wait(block_ready.at[distance - 1], 1)

    for c in range(CHUNKS):
        for i in range(quarter):
            for source in others:
                rs_copy(source, source, i, c).wait_recv()
            head = chip * quarter + i
            total = rs_in[kth(0), i, span(c)]
            for k in range(1, CHIPS):
                total = chip_decay(kth(k), head) * total + rs_in[kth(k), i, span(c)]
            blk_out[i, pl.ds(LEAD + c * PIECE, PIECE)] = total
            if c == 0:
                across = chip_decay(0, head)
                for k in range(1, CHIPS):
                    across = across * chip_decay(k, head)
                blk_out[i, 0:LEAD] = jnp.broadcast_to(across, (LEAD, LANES))
            for distance in range(1, blocks):
                pl.when(sends_to(distance))(blk_copy(distance, i, c).start)

    for c in range(CHUNKS):
        for i in range(quarter):
            entering = jnp.zeros((PIECE, HEAD_DIM), F32)
            for distance in range(blocks - 1, 0, -1):
                hears = hears_from(distance)
                pl.when(hears)(blk_copy(distance, i, c).wait_recv)

                @pl.when(jnp.logical_not(hears))
                def _():
                    blk_in[distance - 1, i, block_span(c)] = jnp.zeros(
                        (PIECE + (LEAD if c == 0 else 0), HEAD_DIM), F32
                    )

                entering = (
                    blk_in[distance - 1, i, 0:1] * entering
                    + blk_in[distance - 1, i, pl.ds(LEAD + c * PIECE, PIECE)]
                )
            head = chip * quarter + i
            for k in range(CHIPS):
                ag_out[kth(k), i, span(c)] = entering
                if k < CHIPS - 1:
                    entering = chip_decay(kth(k), head) * entering + rs_in[kth(k), i, span(c)]
            for target in others:
                ag_copy(target, chip, i, c).start()

    for whose, i in ((whose, i) for whose in (chip, beside, above, opposite) for i in range(quarter)):
        head = whose * quarter + i
        if whose is chip:
            state_ref[core, head] = ag_out[chip, i]
        else:
            for c in range(CHUNKS):
                ag_copy(whose, whose, i, c).wait_recv()
        back_out[head] = decay_of(place, head) * state_ref[core, head] + part_ref[core, head]
        back_copy(head).start()

    def finish_state():
        for head in range(heads):
            lanes = head_lanes(head)
            query, grad = x_ref[1, :, lanes], x_ref[3, :, lanes]
            upper, lower = halves(state_ref[0, head])
            carried = (dot(grad, upper, (1, 1)) + dot(grad, lower, (1, 1))) * column(heads + head)
            gq_ref[:, lanes] = (iq_ref[:, lanes] + carried).astype(BF16)
            inflow = jnp.sum(query.astype(F32) * carried, axis=1, keepdims=True)
            flow_ref[...] += jnp.where(lane_id == head, inflow, 0.0)

    def finish_back():
        for head in range(heads):
            lanes = head_lanes(head)
            key, value = x_ref[0, :, lanes], x_ref[2, :, lanes]
            upper, lower = halves(state_ref[1, head])
            leave = column(head)
            carried = (dot(key, upper, (1, 0)) + dot(key, lower, (1, 0))) * leave
            gv_ref[:, lanes] = (iv_ref[:, lanes] + carried).astype(BF16)
            outflow = jnp.sum(value.astype(F32) * carried, axis=1, keepdims=True)
            flow_ref[...] -= jnp.where(lane_id == head, outflow, 0.0)
            total = jnp.sum(outflow, axis=0, keepdims=True)
            down_ref[heads + head:heads + head + 1] = jnp.broadcast_to(total, (1, rows))

    def finish_keys():
        for head in range(heads):
            lanes = head_lanes(head)
            carried = dot(x_ref[2, :, lanes], state_ref[1, head].astype(BF16), (1, 1)) * column(head)
            gk_ref[:, lanes] = (ik_ref[:, lanes] + carried).astype(BF16)

    pl.when(core == 0)(finish_state)
    pl.when(core == 1)(finish_back)
    remote(back_out, state_ref.at[1 - core], back_send, back_recv, seq=mate).wait_recv()
    pl.when(core == 0)(finish_back)
    pl.when(core == 1)(finish_state)

    turned = flow_ref[...].T[0:heads]
    wholes = [
        jnp.sum(jnp.sum(state_ref[0, head] * state_ref[1, head], axis=0, keepdims=True), axis=1, keepdims=True)
        for head in range(heads)
    ]
    end_term = through * jnp.concatenate(wholes, axis=0) + down_ref[heads:2 * heads]
    row_lane = lax.broadcasted_iota(jnp.int32, (heads, rows), 1)
    grad_cumul = turned - down_ref[0:heads] + jnp.where(row_lane == rows - 1, end_term, 0.0)
    grad_log = unstacked(dot(stacked(grad_cumul), upto_ref[...], (1, 1)))
    grad_gate = grad_log * (1.0 / (1.0 + jnp.exp(gate_rows))) / 16.0
    pieces = stacked(grad_gate)
    spread = unstacked(dot(pieces, tiled_ref[...], (1, 1)))
    lane = lax.broadcasted_iota(jnp.int32, (heads, LANES), 1)
    owner = lax.broadcasted_iota(jnp.int32, (heads, LANES), 0)
    gw_slots[flat] = jnp.sum(
        jnp.where(lax.div(lane, rank) == owner, spread, 0.0), axis=0, keepdims=True
    )
    weight = weight_ref[...]
    lat_slots[my_head] = (
        dot(weight, pieces[0:heads], (0, 0)) + dot(weight, pieces[pad:pad + heads], (0, 0))
    ) + dot(weight, pieces[2 * pad:2 * pad + heads], (0, 0))

    for distance in range(1, head_devices):

        @pl.when(my_head + distance < head_devices)
        def _():
            pl.semaphore_wait(head_ready.at[distance - 1], 1)

    for away in range(1, members):
        remote(
            gw_slots.at[flat], gw_slots.at[flat], gw_send, gw_recv,
            **member(lax.rem(flat + away, members)),
        ).start()
    for away in range(1, head_devices):
        remote(
            lat_slots.at[my_head], lat_slots.at[my_head], lat_send, lat_recv,
            head=lax.rem(my_head + away, head_devices),
        ).start()

    finish_keys()
    peer = {"head": lax.rem(my_head + 1, head_devices)}
    if head_devices > 1:
        passed = lat_slots.at[pl.ds(0, head_devices - 1)]
        lats = remote(passed, passed, lat_send, lat_recv, **peer)
        lats.wait_recv()
    total = lat_slots[0]
    for slot in range(1, head_devices):
        total = total + lat_slots[slot]
    glat_ref[...] = total
    passed = gw_slots.at[pl.ds(0, members - 1)]
    sums = remote(passed, passed, gw_send, gw_recv, seq=mate)
    sums.wait_recv()
    total = gw_slots[0]
    for slot in range(1, members):
        total = total + gw_slots[slot]
    gw_ref[...] = total

    passed = t_ref.at[pl.ds(0, layer - 1)]
    remote(passed, passed, t_send, t_recv.at[0], seq=mate).wait_send()
    remote(mate_in, mate_in, mate_send, mate_recv.at[0], seq=mate).wait_send()
    passed = rs_out.at[pl.ds(0, CHIPS - 1)]
    remote(passed, passed, rs_send, rs_recv.at[0, 0], seq=mate).wait_send()
    passed = ag_out.at[pl.ds(0, CHIPS - 1)]
    remote(passed, passed, ag_send, ag_recv.at[0, 0], seq=mate).wait_send()
    remote(back_out, back_out, back_send, back_recv, seq=mate).wait_send()
    for distance in range(1, blocks):
        pl.when(sends_to(distance))(
            remote(
                blk_out, blk_out, blk_send.at[distance - 1], blk_recv.at[0, 0], seq=mate
            ).wait_send
        )
    if head_devices > 1:
        lats.wait_send()
    sums.wait_send()


def emit_kernel(gq, gk, gv, glat, gw, oq, ok, ov, olat, ow, sems):
    copies = [
        pltpu.make_async_copy(source, target, sems.at[index])
        for index, (source, target) in enumerate(((gq, oq), (gk, ok), (gv, ov)))
    ]
    for copy in copies:
        copy.start()
    olat[...] = glat[...]
    for head in range(ow.shape[0]):
        ow[head:head + 1] = gw[:, head * ow.shape[1]:(head + 1) * ow.shape[1]]
    for copy in copies:
        copy.wait()


def emit(results, rows, width, rank, heads):
    vmem = pl.BlockSpec(memory_space=pltpu.VMEM)
    hbm = pl.BlockSpec(memory_space=pl.ANY)
    wide = jax.ShapeDtypeStruct((rows, width), BF16)
    return pl.pallas_call(
        emit_kernel,
        out_shape=(
            wide, wide, wide,
            jax.ShapeDtypeStruct((rank, rows), F32), jax.ShapeDtypeStruct((heads, rank), F32),
        ),
        in_specs=[vmem] * 5,
        out_specs=(hbm, hbm, hbm, vmem, vmem),
        scratch_shapes=[pltpu.SemaphoreType.DMA((3,))],
        name="emit",
    )(*(pltpu.with_memory_space_constraint(result, pltpu.VMEM) for result in results))


def on_device(sizes, *args):
    queries, keys_in, values, grad_out, latent, gate_weight, gate_bias, doc_starts, block_docs = args
    rows, width = queries.shape[1], queries.shape[2]
    rank = latent.shape[2]
    seq_count, dp_count, head_devices = sizes
    heads = width // HEAD_DIM
    quarter = heads // CHIPS
    layer = PAIR * CHIPS
    far = max(1, seq_count // layer - 1)
    members = seq_count * dp_count
    pad = -(-heads // 8) * 8
    square = lambda *lead: pltpu.VMEM((*lead, HEAD_DIM, HEAD_DIM), F32)
    dma = lambda *shape: pltpu.SemaphoreType.DMA(shape)
    single = pltpu.SemaphoreType.DMA
    hbm = pl.BlockSpec(memory_space=pltpu.HBM)
    wide = pltpu.VMEM((rows, width), BF16)
    results = pl.pallas_call(
        functools.partial(kernel, (seq_count, dp_count, head_devices, heads)),
        out_shape=(
            wide, wide, wide, pltpu.VMEM((rank, rows), F32), pltpu.VMEM((1, LANES), F32),
        ),
        in_specs=[hbm] * 8,
        scratch_shapes=[
            pltpu.VMEM((4, rows, width), BF16),
            pltpu.VMEM((rank, rows), BF16),
            pltpu.VMEM((heads, rank), BF16),
            pltpu.VMEM((1, heads), F32),
            pltpu.VMEM(doc_starts.shape, jnp.int32),
            pltpu.VMEM((LANES, rows), BF16),
            pltpu.VMEM((3 * pad, rows), F32),
            pltpu.VMEM((LANES, rows), F32),
            pltpu.VMEM((rows, LANES), F32),
            pltpu.VMEM((rows, rows), BF16),
            pltpu.VMEM((rows, width), F32),
            pltpu.VMEM((rows, width), F32),
            pltpu.VMEM((rows, width), F32),
            pltpu.VMEM((rows, LANES), F32),
            pltpu.VMEM((2 * pad, rows), F32),
            pltpu.VMEM((layer, 8, LANES), F32),
            square(2, heads), square(heads), square(CHIPS, quarter), square(CHIPS, quarter),
            pltpu.VMEM((quarter, LEAD + HEAD_DIM, HEAD_DIM), F32),
            pltpu.VMEM((far, quarter, LEAD + HEAD_DIM, HEAD_DIM), F32),
            square(CHIPS, quarter), square(heads), square(2, heads),
            pltpu.VMEM((head_devices, rank, rows), F32),
            pltpu.VMEM((members, 1, LANES), F32),
            dma(4), dma(4), single, dma(2), single, dma(heads), single, dma(CHIPS, CHUNKS),
            dma(far), dma(far, CHUNKS), single, dma(CHIPS, CHUNKS), single, single,
            single, single, single, single,
            pltpu.SemaphoreType.REGULAR((far,)),
            pltpu.SemaphoreType.REGULAR((max(1, head_devices - 1),)),
        ],
        compiler_params=pltpu.CompilerParams(collective_id=0, has_side_effects=True),
        name="gated_backward",
    )(
        keys_in[0], queries[0], values[0], grad_out[0], latent[0].T, gate_weight.T,
        gate_bias[None, :], doc_starts,
    )
    out = emit(results, rows, width, rank, heads)
    return out[0][None], out[1][None], out[2][None], out[3].T[None], out[4].T


def solution(mesh):
    sizes = (mesh.shape["seq"], mesh.shape["dp"], mesh.shape["head"])
    return jax.shard_map(
        functools.partial(on_device, sizes),
        mesh=mesh,
        in_specs=(
            P(("groups", "dp"), "seq", "head"),
            P(("groups", "dp"), "seq", "head"),
            P(("groups", "dp"), "seq", "head"),
            P(("groups", "dp"), "seq", "head"),
            P(("groups", "dp"), "seq", None),
            P(None, "head"),
            P("head"),
            P(("groups", "dp"), None),
            P(("groups", "dp"), "seq"),
        ),
        out_specs=(
            P(("groups", "dp"), "seq", "head"),
            P(("groups", "dp"), "seq", "head"),
            P(("groups", "dp"), "seq", "head"),
            P(("groups", "dp"), "seq", None),
            P("groups", "head"),
        ),
        check_vma=False,
    )
```

```python
import functools
import math

import jax
import jax.numpy as jnp
from jax import lax
from jax.experimental import pallas as pl
from jax.experimental.pallas import tpu as pltpu
from jax.sharding import PartitionSpec as P

HEAD_DIM = 128
LANES = 128
PAIR = 2
CHIPS = 4
LEAD = 8
CHUNKS = 4
PIECE = HEAD_DIM // CHUNKS

MESH = pl.DeviceIdType.MESH
F32 = jnp.float32
BF16 = jnp.bfloat16


def dot(left, right, over):
    return lax.dot_general(
        left, right, (((over[0],), (over[1],)), ((), ())), preferred_element_type=F32,
    )


def halves(tensor):
    upper = tensor.astype(BF16)
    return upper, (tensor - upper.astype(F32)).astype(BF16)


def thirds(tensor):
    upper, rest = tensor.astype(BF16), None
    rest = tensor - upper.astype(F32)
    middle = rest.astype(BF16)
    return upper.astype(F32), middle.astype(F32), rest - middle.astype(F32)


def kernel(
    sizes,
    k_hbm, q_hbm, v_hbm, g_hbm, latent_hbm, weight_hbm, bias_hbm, bounds_hbm,
    gq_ref, gk_ref, gv_ref, glat_ref, gw_ref,
    x_ref, latent_ref, weight_ref, bias_ref, bounds_ref,
    tiled_ref, stack_ref, rows_ref, cols_ref, upto_ref, iq_ref, ik_ref, iv_ref, flow_ref, down_ref,
    t_ref, part_ref, mate_in, rs_out, rs_in, blk_out, blk_in, ag_out, back_out, state_ref,
    lat_slots, gw_slots,
    load_sem, small_sem, t_send, t_recv, mate_send, mate_recv, rs_send, rs_recv,
    blk_send, blk_recv, ag_send, ag_recv, back_send, back_recv,
    lat_send, lat_recv, gw_send, gw_recv, block_ready, head_ready,
):
    seq_count, dp_count, head_devices, heads = sizes
    rows = x_ref.shape[1]
    quarter = heads // CHIPS
    layer = PAIR * CHIPS
    blocks = seq_count // layer
    rank = latent_ref.shape[0]
    pad = stack_ref.shape[0] // 3
    scaling = 1.0 / math.sqrt(HEAD_DIM)
    me = lax.axis_index("seq")
    my_dp = lax.axis_index("dp")
    my_head = lax.axis_index("head")
    core = lax.rem(me, PAIR)
    chip = lax.rem(lax.div(me, PAIR), CHIPS)
    block = lax.div(me, layer)
    group = block * layer
    place = core + PAIR * chip
    mate = me + 1 - 2 * core
    members = seq_count * dp_count
    flat = me * dp_count + my_dp
    beside = chip + 1 - 2 * lax.rem(chip, 2)
    above = chip + 2 - 4 * lax.div(chip, 2)
    opposite = CHIPS - 1 - chip
    others = (opposite, above, beside)

    def at_chip(index):
        return group + index * PAIR + core

    def at_block(distance):
        return me + jnp.where(core == 0, distance, -distance) * layer

    def sends_to(distance):
        return jnp.where(core == 0, block + distance < blocks, block >= distance)

    def hears_from(distance):
        return jnp.where(core == 0, block >= distance, block + distance < blocks)

    def member(index):
        return {"seq": lax.div(index, dp_count), "dp": lax.rem(index, dp_count)}

    def greet(semaphore, **where):
        pl.semaphore_signal(semaphore, inc=1, device_id=where, device_id_type=MESH)

    small = [
        pltpu.make_async_copy(source, target, small_sem.at[index])
        for index, (source, target) in enumerate((
            (latent_hbm, latent_ref), (weight_hbm, weight_ref),
            (bias_hbm, bias_ref), (bounds_hbm, bounds_ref),
        ))
    ]
    loads = [
        pltpu.make_async_copy(source, x_ref.at[index], load_sem.at[index])
        for index, source in enumerate((k_hbm, q_hbm, v_hbm, g_hbm))
    ]
    for copy in small:
        copy.start()

    @pl.when(core == 0)
    def _():
        for index in (1, 3, 0, 2):
            loads[index].start()

    @pl.when(core == 1)
    def _():
        for index in (0, 2, 1, 3):
            loads[index].start()

    barrier = pltpu.get_barrier_semaphore()
    greeted = layer - 1 + seq_count * (dp_count - 1)
    for away in range(1, layer):
        greet(barrier, seq=group + lax.rem(place + away, layer))
    for away in range(1, dp_count):
        for there in range(seq_count):
            greet(barrier, seq=there, dp=lax.rem(my_dp + away, dp_count))
    for distance in range(1, blocks):

        @pl.when(block + distance < blocks)
        def _():
            greet(barrier, seq=me + distance * layer)

        greeted = greeted + jnp.where(block >= distance, 1, 0)
    for distance in range(1, head_devices):

        @pl.when(my_head + distance < head_devices)
        def _():
            greet(barrier, head=my_head + distance)

        greeted = greeted + jnp.where(my_head >= distance, 1, 0)

    row_id = lax.broadcasted_iota(jnp.int32, (rows, rows), 0)
    col_id = lax.broadcasted_iota(jnp.int32, (rows, rows), 1)
    upto_ref[...] = (row_id <= col_id).astype(F32).astype(BF16)
    stack_ref[...] = jnp.zeros_like(stack_ref)
    rows_ref[...] = jnp.zeros_like(rows_ref)
    flow_ref[...] = jnp.zeros_like(flow_ref)

    def stacked(tensor):
        for index, piece in enumerate(thirds(tensor)):
            stack_ref[index * pad:index * pad + heads] = piece
        return stack_ref[...].astype(BF16)

    def unstacked(tensor):
        return (tensor[0:heads] + tensor[pad:pad + heads]) + tensor[2 * pad:2 * pad + heads]

    for copy in small:
        copy.wait()
    gate_rows = dot(weight_ref[...], latent_ref[...], (1, 0))
    eye = lax.broadcasted_iota(jnp.int32, (heads, heads), 0) == lax.broadcasted_iota(
        jnp.int32, (heads, heads), 1
    )
    bias = jnp.sum(jnp.where(eye, bias_ref[...], 0.0), axis=1, keepdims=True)
    gate_rows = gate_rows + bias
    log_decay = (jnp.minimum(gate_rows, 0.0) - jnp.log1p(jnp.exp(-jnp.abs(gate_rows)))) / 16.0
    cumul = unstacked(dot(stacked(log_decay), upto_ref[...], (1, 0)))
    first_pos = me * rows
    bounds = bounds_ref[...]
    position = first_pos + lax.broadcasted_iota(jnp.int32, (rows, bounds.shape[1]), 0)
    opened = jnp.where((bounds >= first_pos) & (bounds <= position), 1.0, 0.0).astype(BF16)
    docs = dot(jnp.ones((8, bounds.shape[1]), BF16), opened, (1, 1))
    doc_row = docs[0:1]
    doc_last = doc_row[:, rows - 1:]
    ending = cumul[:, rows - 1:]
    through = jnp.where(doc_last == 0.0, jnp.exp(ending), 0.0)
    rows_ref[0:heads] = jnp.where(doc_row == doc_last, jnp.exp(ending - cumul), 0.0)
    rows_ref[heads:2 * heads] = jnp.where(doc_row == 0.0, jnp.exp(cumul), 0.0) * scaling
    rows_ref[2 * heads:3 * heads] = cumul
    rows_ref[3 * heads:3 * heads + 8] = docs
    t_ref[place, 0:heads] = jnp.broadcast_to(through, (heads, LANES))

    def column(index):
        return cols_ref[:, index:index + 1]

    def head_lanes(index):
        return pl.ds(index * HEAD_DIM, HEAD_DIM)

    def remote(source, target, send_sem, recv_sem, **where):
        return pltpu.make_async_remote_copy(
            src_ref=source, dst_ref=target, send_sem=send_sem, recv_sem=recv_sem,
            device_id=where, device_id_type=MESH,
        )

    pl.semaphore_wait(barrier, greeted)
    for distance in range(1, blocks):

        @pl.when(block >= distance)
        def _():
            greet(block_ready.at[distance - 1], seq=me - distance * layer)

    for distance in range(1, head_devices):

        @pl.when(my_head >= distance)
        def _():
            greet(head_ready.at[distance - 1], head=my_head - distance)


    def decay_copy(target, slot):
        return remote(
            t_ref.at[slot], t_ref.at[slot], t_send,
            t_recv.at[0 if target is mate else 1], seq=target,
        )

    decay_copy(mate, place).start()
    for whose in others:
        for peer in range(PAIR):
            decay_copy(group + whose * PAIR + peer, place).start()

    def mate_copy(head):
        return remote(
            part_ref.at[1 - core, head], mate_in.at[head], mate_send, mate_recv.at[head], seq=mate
        )

    def span(c):
        return pl.ds(c * PIECE, PIECE)

    def block_span(c):
        return pl.ds(0, LEAD + PIECE) if c == 0 else pl.ds(LEAD + c * PIECE, PIECE)

    def rs_copy(target, source, i, c):
        return remote(
            rs_out.at[target, i, span(c)], rs_in.at[source, i, span(c)],
            rs_send, rs_recv.at[c], seq=at_chip(target),
        )

    def blk_copy(distance, i, c):
        return remote(
            blk_out.at[i, block_span(c)], blk_in.at[distance - 1, i, block_span(c)],
            blk_send.at[distance - 1], blk_recv.at[distance - 1, c], seq=at_block(distance),
        )

    def ag_copy(target, source, i, c):
        return remote(
            ag_out.at[target, i, span(c)], state_ref.at[core, source * quarter + i, span(c)],
            ag_send, ag_recv.at[source], seq=at_chip(target),
        )

    def back_copy(head):
        return remote(
            back_out.at[head], state_ref.at[core, head], back_send, back_recv, seq=mate
        )

    order = [(whose, i) for whose in (*others, chip) for i in range(quarter)]

    def part(way, head):
        lanes = pl.ds(pl.multiple_of(head * HEAD_DIM, HEAD_DIM), HEAD_DIM)
        turned = x_ref[way, :, lanes].astype(F32).T
        upper, lower = halves(turned * rows_ref[pl.ds(way * heads + head, 1)])
        right = x_ref[2 + way, :, lanes]
        part_ref[way, head] = dot(upper, right, (1, 0)) + dot(lower, right, (1, 0))

    def load_wait(way):
        for index in (way, 2 + way):
            pltpu.make_async_copy(k_hbm, x_ref.at[index], load_sem.at[index]).wait()

    load_wait(1 - core)
    for first in range(0, heads, 4):
        batch = [whose * quarter + i for whose, i in order[first:first + 4]]
        for head in batch:
            part(1 - core, head)
        for head in batch:
            mate_copy(head).start()
    load_wait(core)
    for whose, i in order:
        part(core, whose * quarter + i)

    decay_copy(mate, place).wait_recv()

    def decay_of(index, head):
        return t_ref[index, pl.ds(head, 1), :]

    def send_parts():
        for whose, i in order:
            mate_copy(whose * quarter + i).wait_recv()
        for c in range(CHUNKS):
            for whose, i in order:
                head = whose * quarter + i
                keep = decay_of(PAIR * chip + 1 - core, head)
                total = keep * part_ref[core, head, span(c)] + mate_in[head, span(c)]
                if whose is chip:
                    rs_in[chip, i, span(c)] = total
                else:
                    rs_out[whose, i, span(c)] = total
                    rs_copy(whose, chip, i, c).start()

    lane_id = lax.broadcasted_iota(jnp.int32, (rows, LANES), 1)

    def local_head(head):
        lanes = head_lanes(head)
        key, query, value, grad = (x_ref[index, :, lanes] for index in range(4))
        same_doc = (row_id >= col_id) & (column(3 * heads) == rows_ref[3 * heads:3 * heads + 1])
        spread = jnp.where(
            same_doc, column(2 * heads + head) - rows_ref[2 * heads + head:2 * heads + head + 1], 0.0
        )
        weights = jnp.where(same_doc, jnp.exp(spread), 0.0)
        scores = dot(query, key, (1, 1)) * scaling * weights
        pair_dots = dot(grad, value, (1, 1))
        weighted = (pair_dots * weights * scaling).astype(BF16)
        products = scores * pair_dots
        iv_ref[:, lanes] = dot(scores.astype(BF16), grad, (0, 0))
        iq_ref[:, lanes] = dot(weighted, key, (1, 0))
        ik_ref[:, lanes] = dot(weighted, query, (0, 0))
        flow_ref[...] += jnp.where(
            lane_id == head, jnp.sum(products, axis=1, keepdims=True), 0.0
        )
        down_ref[head:head + 1] = jnp.sum(products, axis=0, keepdims=True)

    passes_on = sends_to(1)
    pl.when(passes_on)(send_parts)
    for index in range(LANES // rank):
        tiled_ref[index * rank:(index + 1) * rank] = latent_ref[...]
    cols_ref[...] = rows_ref[...].T
    for head in range(heads):
        local_head(head)
    pl.when(jnp.logical_not(passes_on))(send_parts)

    def kth(k):
        return jnp.where(core == 0, k, CHIPS - 1 - k)

    def chip_decay(index, head):
        return decay_of(PAIR * index, head) * decay_of(PAIR * index + 1, head)

    passed = t_ref.at[pl.ds(0, layer - PAIR)]
    remote(passed, passed, t_send, t_recv.at[1], seq=mate).wait_recv()
    for distance in range(1, blocks):

        @pl.when(block + distance < blocks)
        def _():
            pl.semaphore_wait(block_ready.at[distance - 1], 1)

    for c in range(CHUNKS):
        passed = rs_in.at[pl.ds(0, CHIPS - 1), :, span(c)]
        remote(passed, passed, rs_send, rs_recv.at[c], seq=mate).wait_recv()
        for i in range(quarter):
            head = chip * quarter + i
            total = rs_in[kth(0), i, span(c)]
            for k in range(1, CHIPS):
                total = chip_decay(kth(k), head) * total + rs_in[kth(k), i, span(c)]
            blk_out[i, pl.ds(LEAD + c * PIECE, PIECE)] = total
            if c == 0:
                across = chip_decay(0, head)
                for k in range(1, CHIPS):
                    across = across * chip_decay(k, head)
                blk_out[i, 0:LEAD] = jnp.broadcast_to(across, (LEAD, LANES))
            for distance in range(1, blocks):
                pl.when(sends_to(distance))(blk_copy(distance, i, c).start)

    for c in range(CHUNKS):
        for i in range(quarter):
            entering = jnp.zeros((PIECE, HEAD_DIM), F32)
            for distance in range(blocks - 1, 0, -1):
                hears = hears_from(distance)
                pl.when(hears)(blk_copy(distance, i, c).wait_recv)

                @pl.when(jnp.logical_not(hears))
                def _():
                    blk_in[distance - 1, i, block_span(c)] = jnp.zeros(
                        (PIECE + (LEAD if c == 0 else 0), HEAD_DIM), F32
                    )

                entering = (
                    blk_in[distance - 1, i, 0:1] * entering
                    + blk_in[distance - 1, i, pl.ds(LEAD + c * PIECE, PIECE)]
                )
            head = chip * quarter + i
            for k in range(CHIPS):
                ag_out[kth(k), i, span(c)] = entering
                if k < CHIPS - 1:
                    entering = chip_decay(kth(k), head) * entering + rs_in[kth(k), i, span(c)]
            for target in others:
                ag_copy(target, chip, i, c).start()

    for whose in (chip, beside, above, opposite):
        mine = pl.ds(whose * quarter, quarter)
        if whose is not chip:
            remote(
                ag_out.at[whose], state_ref.at[core, mine], ag_send, ag_recv.at[whose], seq=mate
            ).wait_recv()
        for i in range(quarter):
            head = whose * quarter + i
            if whose is chip:
                state_ref[core, head] = ag_out[chip, i]
            back_out[head] = decay_of(place, head) * state_ref[core, head] + part_ref[core, head]
            back_copy(head).start()

    def finish_state():
        for head in range(heads):
            lanes = head_lanes(head)
            query, grad = x_ref[1, :, lanes], x_ref[3, :, lanes]
            upper, lower = halves(state_ref[0, head])
            carried = (dot(grad, upper, (1, 1)) + dot(grad, lower, (1, 1))) * column(heads + head)
            gq_ref[:, lanes] = (iq_ref[:, lanes] + carried).astype(BF16)
            inflow = jnp.sum(query.astype(F32) * carried, axis=1, keepdims=True)
            flow_ref[...] += jnp.where(lane_id == head, inflow, 0.0)

    def finish_back():
        for head in range(heads):
            lanes = head_lanes(head)
            key, value = x_ref[0, :, lanes], x_ref[2, :, lanes]
            upper, lower = halves(state_ref[1, head])
            leave = column(head)
            carried = (dot(key, upper, (1, 0)) + dot(key, lower, (1, 0))) * leave
            gv_ref[:, lanes] = (iv_ref[:, lanes] + carried).astype(BF16)
            outflow = jnp.sum(value.astype(F32) * carried, axis=1, keepdims=True)
            flow_ref[...] -= jnp.where(lane_id == head, outflow, 0.0)
            total = jnp.sum(outflow, axis=0, keepdims=True)
            down_ref[heads + head:heads + head + 1] = jnp.broadcast_to(total, (1, rows))

    def finish_keys():
        for head in range(heads):
            lanes = head_lanes(head)
            carried = dot(x_ref[2, :, lanes], state_ref[1, head].astype(BF16), (1, 1)) * column(head)
            gk_ref[:, lanes] = (ik_ref[:, lanes] + carried).astype(BF16)

    pl.when(core == 0)(finish_state)
    pl.when(core == 1)(finish_back)
    remote(back_out, state_ref.at[1 - core], back_send, back_recv, seq=mate).wait_recv()
    pl.when(core == 0)(finish_back)
    pl.when(core == 1)(finish_state)

    turned = flow_ref[...].T[0:heads]
    wholes = [
        jnp.sum(jnp.sum(state_ref[0, head] * state_ref[1, head], axis=0, keepdims=True), axis=1, keepdims=True)
        for head in range(heads)
    ]
    end_term = through * jnp.concatenate(wholes, axis=0) + down_ref[heads:2 * heads]
    row_lane = lax.broadcasted_iota(jnp.int32, (heads, rows), 1)
    grad_cumul = turned - down_ref[0:heads] + jnp.where(row_lane == rows - 1, end_term, 0.0)
    grad_log = unstacked(dot(stacked(grad_cumul), upto_ref[...], (1, 1)))
    grad_gate = grad_log * (1.0 / (1.0 + jnp.exp(gate_rows))) / 16.0
    pieces = stacked(grad_gate)
    spread = unstacked(dot(pieces, tiled_ref[...], (1, 1)))
    lane = lax.broadcasted_iota(jnp.int32, (heads, LANES), 1)
    owner = lax.broadcasted_iota(jnp.int32, (heads, LANES), 0)
    gw_slots[flat] = jnp.sum(
        jnp.where(lax.div(lane, rank) == owner, spread, 0.0), axis=0, keepdims=True
    )
    weight = weight_ref[...]
    lat_slots[my_head] = (
        dot(weight, pieces[0:heads], (0, 0)) + dot(weight, pieces[pad:pad + heads], (0, 0))
    ) + dot(weight, pieces[2 * pad:2 * pad + heads], (0, 0))

    for distance in range(1, head_devices):

        @pl.when(my_head + distance < head_devices)
        def _():
            pl.semaphore_wait(head_ready.at[distance - 1], 1)

    for away in range(1, members):
        remote(
            gw_slots.at[flat], gw_slots.at[flat], gw_send, gw_recv,
            **member(lax.rem(flat + away, members)),
        ).start()
    for away in range(1, head_devices):
        remote(
            lat_slots.at[my_head], lat_slots.at[my_head], lat_send, lat_recv,
            head=lax.rem(my_head + away, head_devices),
        ).start()

    finish_keys()
    peer = {"head": lax.rem(my_head + 1, head_devices)}
    if head_devices > 1:
        passed = lat_slots.at[pl.ds(0, head_devices - 1)]
        lats = remote(passed, passed, lat_send, lat_recv, **peer)
        lats.wait_recv()
    total = lat_slots[0]
    for slot in range(1, head_devices):
        total = total + lat_slots[slot]
    glat_ref[...] = total
    passed = gw_slots.at[pl.ds(0, members - 1)]
    sums = remote(passed, passed, gw_send, gw_recv, seq=mate)
    sums.wait_recv()
    total = gw_slots[0]
    for slot in range(1, members):
        total = total + gw_slots[slot]
    gw_ref[...] = total

    passed = t_ref.at[pl.ds(0, layer - 1)]
    remote(passed, passed, t_send, t_recv.at[0], seq=mate).wait_send()
    remote(mate_in, mate_in, mate_send, mate_recv.at[0], seq=mate).wait_send()
    passed = rs_out.at[pl.ds(0, CHIPS - 1)]
    remote(passed, passed, rs_send, rs_recv.at[0], seq=mate).wait_send()
    passed = ag_out.at[pl.ds(0, CHIPS - 1)]
    remote(passed, passed, ag_send, ag_recv.at[0], seq=mate).wait_send()
    remote(back_out, back_out, back_send, back_recv, seq=mate).wait_send()
    for distance in range(1, blocks):
        pl.when(sends_to(distance))(
            remote(
                blk_out, blk_out, blk_send.at[distance - 1], blk_recv.at[0, 0], seq=mate
            ).wait_send
        )
    if head_devices > 1:
        lats.wait_send()
    sums.wait_send()


def emit_kernel(gq, gk, gv, glat, gw, oq, ok, ov, olat, ow):
    oq[...] = gq[...]
    ok[...] = gk[...]
    ov[...] = gv[...]
    olat[...] = glat[...]
    for head in range(ow.shape[0]):
        ow[head:head + 1] = gw[:, head * ow.shape[1]:(head + 1) * ow.shape[1]]


def emit(results, rows, width, rank, heads):
    vmem = pl.BlockSpec(memory_space=pltpu.VMEM)
    hbm = pl.BlockSpec(memory_space=pl.ANY)
    wide = jax.ShapeDtypeStruct((rows, width), BF16)
    return pl.pallas_call(
        emit_kernel,
        out_shape=(
            wide, wide, wide,
            jax.ShapeDtypeStruct((rank, rows), F32), jax.ShapeDtypeStruct((heads, rank), F32),
        ),
        in_specs=[vmem] * 5,
        out_specs=(vmem,) * 5,

        name="emit",
    )(*(pltpu.with_memory_space_constraint(result, pltpu.VMEM) for result in results))


def on_device(sizes, *args):
    queries, keys_in, values, grad_out, latent, gate_weight, gate_bias, doc_starts, block_docs = args
    rows, width = queries.shape[1], queries.shape[2]
    rank = latent.shape[2]
    seq_count, dp_count, head_devices = sizes
    heads = width // HEAD_DIM
    quarter = heads // CHIPS
    layer = PAIR * CHIPS
    far = max(1, seq_count // layer - 1)
    members = seq_count * dp_count
    pad = -(-heads // 8) * 8
    square = lambda *lead: pltpu.VMEM((*lead, HEAD_DIM, HEAD_DIM), F32)
    dma = lambda *shape: pltpu.SemaphoreType.DMA(shape)
    single = pltpu.SemaphoreType.DMA
    hbm = pl.BlockSpec(memory_space=pltpu.HBM)
    wide = pltpu.VMEM((rows, width), BF16)
    results = pl.pallas_call(
        functools.partial(kernel, (seq_count, dp_count, head_devices, heads)),
        out_shape=(
            wide, wide, wide, pltpu.VMEM((rank, rows), F32), pltpu.VMEM((1, LANES), F32),
        ),
        in_specs=[hbm] * 8,
        scratch_shapes=[
            pltpu.VMEM((4, rows, width), BF16),
            pltpu.VMEM((rank, rows), BF16),
            pltpu.VMEM((heads, rank), BF16),
            pltpu.VMEM((1, heads), F32),
            pltpu.VMEM(doc_starts.shape, jnp.int32),
            pltpu.VMEM((LANES, rows), BF16),
            pltpu.VMEM((3 * pad, rows), F32),
            pltpu.VMEM((LANES, rows), F32),
            pltpu.VMEM((rows, LANES), F32),
            pltpu.VMEM((rows, rows), BF16),
            pltpu.VMEM((rows, width), F32),
            pltpu.VMEM((rows, width), F32),
            pltpu.VMEM((rows, width), F32),
            pltpu.VMEM((rows, LANES), F32),
            pltpu.VMEM((2 * pad, rows), F32),
            pltpu.VMEM((layer, 8, LANES), F32),
            square(2, heads), square(heads), square(CHIPS, quarter), square(CHIPS, quarter),
            pltpu.VMEM((quarter, LEAD + HEAD_DIM, HEAD_DIM), F32),
            pltpu.VMEM((far, quarter, LEAD + HEAD_DIM, HEAD_DIM), F32),
            square(CHIPS, quarter), square(heads), square(2, heads),
            pltpu.VMEM((head_devices, rank, rows), F32),
            pltpu.VMEM((members, 1, LANES), F32),
            dma(4), dma(4), single, dma(2), single, dma(heads), single, dma(CHUNKS),
            dma(far), dma(far, CHUNKS), single, dma(CHIPS), single, single,
            single, single, single, single,
            pltpu.SemaphoreType.REGULAR((far,)),
            pltpu.SemaphoreType.REGULAR((max(1, head_devices - 1),)),
        ],
        compiler_params=pltpu.CompilerParams(collective_id=0, has_side_effects=True),
        name="gated_backward",
    )(
        keys_in[0], queries[0], values[0], grad_out[0], latent[0].T, gate_weight.T,
        gate_bias[None, :], doc_starts,
    )
    out = emit(results, rows, width, rank, heads)
    return out[0][None], out[1][None], out[2][None], out[3].T[None], out[4].T


def solution(mesh):
    sizes = (mesh.shape["seq"], mesh.shape["dp"], mesh.shape["head"])
    return jax.shard_map(
        functools.partial(on_device, sizes),
        mesh=mesh,
        in_specs=(
            P(("groups", "dp"), "seq", "head"),
            P(("groups", "dp"), "seq", "head"),
            P(("groups", "dp"), "seq", "head"),
            P(("groups", "dp"), "seq", "head"),
            P(("groups", "dp"), "seq", None),
            P(None, "head"),
            P("head"),
            P(("groups", "dp"), None),
            P(("groups", "dp"), "seq"),
        ),
        out_specs=(
            P(("groups", "dp"), "seq", "head"),
            P(("groups", "dp"), "seq", "head"),
            P(("groups", "dp"), "seq", "head"),
            P(("groups", "dp"), "seq", None),
            P("groups", "head"),
        ),
        check_vma=False,
    )
```

```python
import functools
import math

import jax
import jax.numpy as jnp
from jax import lax
from jax.experimental import pallas as pl
from jax.experimental.pallas import tpu as pltpu
from jax.sharding import PartitionSpec as P

HEAD_DIM = 128
LANES = 128
PAIR = 2
CHIPS = 4
LEAD = 8
CHUNKS = 4
PIECE = HEAD_DIM // CHUNKS

MESH = pl.DeviceIdType.MESH
F32 = jnp.float32
BF16 = jnp.bfloat16


def dot(left, right, over):
    return lax.dot_general(
        left, right, (((over[0],), (over[1],)), ((), ())), preferred_element_type=F32,
    )


def halves(tensor):
    upper = tensor.astype(BF16)
    return upper, (tensor - upper.astype(F32)).astype(BF16)


def thirds(tensor):
    upper, rest = tensor.astype(BF16), None
    rest = tensor - upper.astype(F32)
    middle = rest.astype(BF16)
    return upper.astype(F32), middle.astype(F32), rest - middle.astype(F32)


def kernel(
    sizes,
    k_hbm, q_hbm, v_hbm, g_hbm, latent_hbm, weight_hbm, bias_hbm, bounds_hbm,
    gq_ref, gk_ref, gv_ref, glat_ref, gw_ref,
    x_ref, latent_ref, weight_ref, bias_ref, bounds_ref,
    tiled_ref, stack_ref, rows_ref, cols_ref, upto_ref, iq_ref, ik_ref, iv_ref, left_ref, value_ref, base_ref, through_ref,
    t_ref, part_ref, mate_in, rs_out, rs_in, blk_out, blk_in, ag_out, back_out, state_ref,
    lat_slots, gw_slots,
    load_sem, small_sem, t_send, t_recv, mate_send, mate_recv, rs_send, rs_recv,
    blk_send, blk_recv, ag_send, ag_recv, back_send, back_recv,
    lat_send, lat_recv, gw_send, gw_recv, block_ready, head_ready,
):
    seq_count, dp_count, head_devices, heads = sizes
    rows = x_ref.shape[1]
    quarter = heads // CHIPS
    layer = PAIR * CHIPS
    blocks = seq_count // layer
    rank = latent_ref.shape[0]
    pad = stack_ref.shape[0] // 3
    scaling = 1.0 / math.sqrt(HEAD_DIM)
    me = lax.axis_index("seq")
    my_dp = lax.axis_index("dp")
    my_head = lax.axis_index("head")
    core = lax.rem(me, PAIR)
    chip = lax.rem(lax.div(me, PAIR), CHIPS)
    block = lax.div(me, layer)
    group = block * layer
    place = core + PAIR * chip
    mate = me + 1 - 2 * core
    members = seq_count * dp_count
    flat = me * dp_count + my_dp
    beside = chip + 1 - 2 * lax.rem(chip, 2)
    above = chip + 2 - 4 * lax.div(chip, 2)
    opposite = CHIPS - 1 - chip
    others = (opposite, above, beside)

    def at_chip(index):
        return group + index * PAIR + core

    def at_block(distance):
        return me + jnp.where(core == 0, distance, -distance) * layer

    def sends_to(distance):
        return jnp.where(core == 0, block + distance < blocks, block >= distance)

    def hears_from(distance):
        return jnp.where(core == 0, block >= distance, block + distance < blocks)

    def member(index):
        return {"seq": lax.div(index, dp_count), "dp": lax.rem(index, dp_count)}

    def greet(semaphore, **where):
        pl.semaphore_signal(semaphore, inc=1, device_id=where, device_id_type=MESH)

    small = [
        pltpu.make_async_copy(source, target, small_sem.at[index])
        for index, (source, target) in enumerate((
            (latent_hbm, latent_ref), (weight_hbm, weight_ref),
            (bias_hbm, bias_ref), (bounds_hbm, bounds_ref),
        ))
    ]
    loads = [
        pltpu.make_async_copy(source, x_ref.at[index], load_sem.at[index])
        for index, source in enumerate((k_hbm, q_hbm, v_hbm, g_hbm))
    ]
    for copy in small:
        copy.start()

    @pl.when(core == 0)
    def _():
        for index in (1, 3, 0, 2):
            loads[index].start()

    @pl.when(core == 1)
    def _():
        for index in (0, 2, 1, 3):
            loads[index].start()

    barrier = pltpu.get_barrier_semaphore()
    greeted = layer - 1 + seq_count * (dp_count - 1)
    for away in range(1, layer):
        greet(barrier, seq=group + lax.rem(place + away, layer))
    for away in range(1, dp_count):
        for there in range(seq_count):
            greet(barrier, seq=there, dp=lax.rem(my_dp + away, dp_count))
    for distance in range(1, blocks):

        @pl.when(block + distance < blocks)
        def _():
            greet(barrier, seq=me + distance * layer)

        greeted = greeted + jnp.where(block >= distance, 1, 0)
    for distance in range(1, head_devices):

        @pl.when(my_head + distance < head_devices)
        def _():
            greet(barrier, head=my_head + distance)

        greeted = greeted + jnp.where(my_head >= distance, 1, 0)

    row_id = lax.broadcasted_iota(jnp.int32, (rows, rows), 0)
    col_id = lax.broadcasted_iota(jnp.int32, (rows, rows), 1)
    upto_ref[...] = (row_id <= col_id).astype(F32).astype(BF16)
    stack_ref[...] = jnp.zeros_like(stack_ref)
    rows_ref[...] = jnp.zeros_like(rows_ref)

    def stacked(tensor):
        for index, piece in enumerate(thirds(tensor)):
            stack_ref[index * pad:index * pad + heads] = piece
        return stack_ref[...].astype(BF16)

    def unstacked(tensor):
        return (tensor[0:heads] + tensor[pad:pad + heads]) + tensor[2 * pad:2 * pad + heads]

    for copy in small:
        copy.wait()
    gate_rows = dot(weight_ref[...], latent_ref[...], (1, 0))
    eye = lax.broadcasted_iota(jnp.int32, (heads, heads), 0) == lax.broadcasted_iota(
        jnp.int32, (heads, heads), 1
    )
    bias = jnp.sum(jnp.where(eye, bias_ref[...], 0.0), axis=1, keepdims=True)
    gate_rows = gate_rows + bias
    log_decay = (jnp.minimum(gate_rows, 0.0) - jnp.log1p(jnp.exp(-jnp.abs(gate_rows)))) / 16.0
    cumul = unstacked(dot(stacked(log_decay), upto_ref[...], (1, 0)))
    first_pos = me * rows
    bounds = bounds_ref[...]
    position = first_pos + lax.broadcasted_iota(jnp.int32, (rows, bounds.shape[1]), 0)
    opened = jnp.where((bounds >= first_pos) & (bounds <= position), 1.0, 0.0).astype(BF16)
    docs = dot(jnp.ones((8, bounds.shape[1]), BF16), opened, (1, 1))
    doc_row = docs[0:1]
    doc_last = doc_row[:, rows - 1:]
    ending = cumul[:, rows - 1:]
    through = jnp.where(doc_last == 0.0, jnp.exp(ending), 0.0)
    rows_ref[0:heads] = jnp.where(doc_row == doc_last, jnp.exp(ending - cumul), 0.0)
    rows_ref[heads:2 * heads] = jnp.where(doc_row == 0.0, jnp.exp(cumul), 0.0) * scaling
    rows_ref[2 * heads:3 * heads] = cumul
    rows_ref[3 * heads:3 * heads + 8] = docs
    t_ref[place, 0:heads] = jnp.broadcast_to(through, (heads, LANES))

    def column(index):
        return cols_ref[:, index:index + 1]

    def head_lanes(index):
        return pl.ds(index * HEAD_DIM, HEAD_DIM)

    def remote(source, target, send_sem, recv_sem, **where):
        return pltpu.make_async_remote_copy(
            src_ref=source, dst_ref=target, send_sem=send_sem, recv_sem=recv_sem,
            device_id=where, device_id_type=MESH,
        )

    pl.semaphore_wait(barrier, greeted)
    for distance in range(1, blocks):

        @pl.when(block >= distance)
        def _():
            greet(block_ready.at[distance - 1], seq=me - distance * layer)

    for distance in range(1, head_devices):

        @pl.when(my_head >= distance)
        def _():
            greet(head_ready.at[distance - 1], head=my_head - distance)


    def decay_copy(target, slot):
        return remote(
            t_ref.at[slot], t_ref.at[slot], t_send,
            t_recv.at[0 if target is mate else 1], seq=target,
        )

    decay_copy(mate, place).start()
    for whose in others:
        for peer in range(PAIR):
            decay_copy(group + whose * PAIR + peer, place).start()

    def mate_copy(head):
        return remote(
            part_ref.at[1 - core, head], mate_in.at[head], mate_send, mate_recv.at[head], seq=mate
        )

    def span(c):
        return pl.ds(c * PIECE, PIECE)

    def block_span(c):
        return pl.ds(0, LEAD + PIECE) if c == 0 else pl.ds(LEAD + c * PIECE, PIECE)

    def rs_copy(target, source, i, c):
        return remote(
            rs_out.at[target, i, span(c)], rs_in.at[source, i, span(c)],
            rs_send, rs_recv.at[c], seq=at_chip(target),
        )

    def blk_copy(distance, i, c):
        return remote(
            blk_out.at[i, block_span(c)], blk_in.at[distance - 1, i, block_span(c)],
            blk_send.at[distance - 1], blk_recv.at[distance - 1, c], seq=at_block(distance),
        )

    def ag_copy(target, source, i, c):
        return remote(
            ag_out.at[target, i, span(c)], state_ref.at[core, source * quarter + i, span(c)],
            ag_send, ag_recv.at[source], seq=at_chip(target),
        )

    def back_copy(head):
        return remote(
            back_out.at[head], state_ref.at[core, head], back_send, back_recv, seq=mate
        )

    order = [(whose, i) for whose in (*others, chip) for i in range(quarter)]

    def part(way, head):
        lanes = pl.ds(pl.multiple_of(head * HEAD_DIM, HEAD_DIM), HEAD_DIM)
        turned = x_ref[way, :, lanes].T
        left_ref[way, head] = turned
        upper, lower = halves(turned.astype(F32) * rows_ref[pl.ds(way * heads + head, 1)])
        right = x_ref[2 + way, :, lanes]
        part_ref[way, head] = dot(upper, right, (1, 0)) + dot(lower, right, (1, 0))

    def load_wait(way):
        for index in (way, 2 + way):
            pltpu.make_async_copy(k_hbm, x_ref.at[index], load_sem.at[index]).wait()

    load_wait(1 - core)
    for first in range(0, heads, 4):
        batch = [whose * quarter + i for whose, i in order[first:first + 4]]
        for head in batch:
            part(1 - core, head)
        for head in batch:
            mate_copy(head).start()
    load_wait(core)
    for whose, i in order:
        part(core, whose * quarter + i)

    decay_copy(mate, place).wait_recv()

    def decay_of(index, head):
        return t_ref[index, pl.ds(head, 1), :]

    def send_parts():
        for whose, i in order:
            head = whose * quarter + i
            keep = decay_of(PAIR * chip + 1 - core, head)
            mate_copy(head).wait_recv()
            total = keep * part_ref[core, head] + mate_in[head]
            if whose is chip:
                rs_in[chip, i] = total
            else:
                rs_out[whose, i] = total
                for c in range(CHUNKS // 2):
                    rs_copy(whose, chip, i, c).start()
        for whose, i in order:
            if whose is not chip:
                for c in range(CHUNKS // 2, CHUNKS):
                    rs_copy(whose, chip, i, c).start()

    lane_id = lax.broadcasted_iota(jnp.int32, (rows, LANES), 1)

    def local_head(head):
        lanes = head_lanes(head)
        key, query, value, grad = (x_ref[index, :, lanes] for index in range(4))
        same_doc = (row_id >= col_id) & (column(3 * heads) == rows_ref[3 * heads:3 * heads + 1])
        spread = jnp.where(
            same_doc, column(2 * heads + head) - rows_ref[2 * heads + head:2 * heads + head + 1], 0.0
        )
        weights = jnp.where(same_doc, jnp.exp(spread), 0.0)
        scores = dot(query, key, (1, 1)) * scaling * weights
        pair_dots = dot(grad, value, (1, 1))
        weighted = (pair_dots * weights * scaling).astype(BF16)
        products = scores * pair_dots
        iv_ref[:, lanes] = dot(scores.astype(BF16), grad, (0, 0))
        iq_ref[:, lanes] = dot(weighted, key, (1, 0))
        ik_ref[:, lanes] = dot(weighted, query, (0, 0))
        flows.append(jnp.sum(products, axis=1, keepdims=True))
        base_ref[head:head + 1] = jnp.sum(products, axis=0, keepdims=True)

    passes_on = sends_to(1)
    pl.when(passes_on)(send_parts)
    for index in range(LANES // rank):
        tiled_ref[index * rank:(index + 1) * rank] = latent_ref[...]
    cols_ref[...] = rows_ref[...].T
    flows = []
    for head in range(heads):
        local_head(head)
    pl.when(jnp.logical_not(passes_on))(send_parts)
    gathered = jnp.zeros((rows, LANES), F32)
    for head in range(heads):
        gathered = jnp.where(lane_id == head, flows[head], gathered)
        value_ref[head] = x_ref[2, :, head_lanes(head)].T
    base_ref[0:heads] = gathered.T[0:heads] - base_ref[0:heads]

    def kth(k):
        return jnp.where(core == 0, k, CHIPS - 1 - k)

    def chip_decay(index, head):
        return decay_of(PAIR * index, head) * decay_of(PAIR * index + 1, head)

    passed = t_ref.at[pl.ds(0, layer - PAIR)]
    remote(passed, passed, t_send, t_recv.at[1], seq=mate).wait_recv()
    for distance in range(1, blocks):

        @pl.when(block + distance < blocks)
        def _():
            pl.semaphore_wait(block_ready.at[distance - 1], 1)

    for c in range(CHUNKS):
        passed = rs_in.at[pl.ds(0, CHIPS - 1), :, span(c)]
        remote(passed, passed, rs_send, rs_recv.at[c], seq=mate).wait_recv()
        for i in range(quarter):
            head = chip * quarter + i
            total = rs_in[kth(0), i, span(c)]
            for k in range(1, CHIPS):
                total = chip_decay(kth(k), head) * total + rs_in[kth(k), i, span(c)]
            blk_out[i, pl.ds(LEAD + c * PIECE, PIECE)] = total
            if c == 0:
                across = chip_decay(0, head)
                for k in range(1, CHIPS):
                    across = across * chip_decay(k, head)
                blk_out[i, 0:LEAD] = jnp.broadcast_to(across, (LEAD, LANES))
            for distance in range(1, blocks):
                pl.when(sends_to(distance))(blk_copy(distance, i, c).start)

    for c in range(CHUNKS):
        for i in range(quarter):
            entering = jnp.zeros((PIECE, HEAD_DIM), F32)
            for distance in range(blocks - 1, 0, -1):
                hears = hears_from(distance)
                pl.when(hears)(blk_copy(distance, i, c).wait_recv)

                @pl.when(jnp.logical_not(hears))
                def _():
                    blk_in[distance - 1, i, block_span(c)] = jnp.zeros(
                        (PIECE + (LEAD if c == 0 else 0), HEAD_DIM), F32
                    )

                entering = (
                    blk_in[distance - 1, i, 0:1] * entering
                    + blk_in[distance - 1, i, pl.ds(LEAD + c * PIECE, PIECE)]
                )
            head = chip * quarter + i
            for k in range(CHIPS):
                ag_out[kth(k), i, span(c)] = entering
                if k < CHIPS - 1:
                    entering = chip_decay(kth(k), head) * entering + rs_in[kth(k), i, span(c)]
            for target in others:
                ag_copy(target, chip, i, c).start()

    for whose in (chip, beside, above, opposite):
        mine = pl.ds(whose * quarter, quarter)
        if whose is not chip:
            remote(
                ag_out.at[whose], state_ref.at[core, mine], ag_send, ag_recv.at[whose], seq=mate
            ).wait_recv()
        for i in range(quarter):
            head = whose * quarter + i
            if whose is chip:
                state_ref[core, head] = ag_out[chip, i]
            back_out[head] = decay_of(place, head) * state_ref[core, head] + part_ref[core, head]
            back_copy(head).start()

    def state_rows():
        for head in range(heads):
            upper, lower = halves(state_ref[0, head])
            grad = x_ref[3, :, head_lanes(head)]
            carried = dot(upper, grad, (1, 1)) + dot(lower, grad, (1, 1))
            inflow = jnp.sum(carried * left_ref[1, head].astype(F32), axis=0, keepdims=True)
            through_ref[head:head + 1] = inflow * rows_ref[heads + head:heads + head + 1]

    def back_rows():
        for head in range(heads):
            upper, lower = halves(state_ref[1, head])
            key = x_ref[0, :, head_lanes(head)]
            carried = dot(upper, key, (0, 1)) + dot(lower, key, (0, 1))
            outflow = jnp.sum(carried * value_ref[head].astype(F32), axis=0, keepdims=True)
            through_ref[pad + head:pad + head + 1] = outflow * rows_ref[head:head + 1]

    def finish_heads():
        for head in range(heads):
            lanes = head_lanes(head)
            key, query, value, grad = (x_ref[index, :, lanes] for index in range(4))
            enter, leave = column(heads + head), column(head)
            upper, lower = halves(state_ref[0, head])
            carried = (dot(grad, upper, (1, 1)) + dot(grad, lower, (1, 1))) * enter
            gq_ref[:, lanes] = (iq_ref[:, lanes] + carried).astype(BF16)
            upper, lower = halves(state_ref[1, head])
            carried = (dot(key, upper, (1, 0)) + dot(key, lower, (1, 0))) * leave
            gv_ref[:, lanes] = (iv_ref[:, lanes] + carried).astype(BF16)
            carried = dot(value, upper, (1, 1)) * leave
            gk_ref[:, lanes] = (ik_ref[:, lanes] + carried).astype(BF16)

    pl.when(core == 0)(state_rows)
    pl.when(core == 1)(back_rows)
    remote(back_out, state_ref.at[1 - core], back_send, back_recv, seq=mate).wait_recv()
    pl.when(core == 0)(back_rows)
    pl.when(core == 1)(state_rows)

    wholes = [
        jnp.sum(jnp.sum(state_ref[0, head] * state_ref[1, head], axis=0, keepdims=True), axis=1, keepdims=True)
        for head in range(heads)
    ]
    inflow, outflow = through_ref[0:heads], through_ref[pad:pad + heads]
    end_term = through * jnp.concatenate(wholes, axis=0) + jnp.sum(outflow, axis=1, keepdims=True)
    row_lane = lax.broadcasted_iota(jnp.int32, (heads, rows), 1)
    grad_cumul = base_ref[0:heads] + (inflow - outflow) + jnp.where(
        row_lane == rows - 1, end_term, 0.0
    )
    grad_log = unstacked(dot(stacked(grad_cumul), upto_ref[...], (1, 1)))
    grad_gate = grad_log * (1.0 / (1.0 + jnp.exp(gate_rows))) / 16.0
    pieces = stacked(grad_gate)
    spread = unstacked(dot(pieces, tiled_ref[...], (1, 1)))
    lane = lax.broadcasted_iota(jnp.int32, (heads, LANES), 1)
    owner = lax.broadcasted_iota(jnp.int32, (heads, LANES), 0)
    gw_slots[flat] = jnp.sum(
        jnp.where(lax.div(lane, rank) == owner, spread, 0.0), axis=0, keepdims=True
    )
    weight = weight_ref[...]
    lat_slots[my_head] = (
        dot(weight, pieces[0:heads], (0, 0)) + dot(weight, pieces[pad:pad + heads], (0, 0))
    ) + dot(weight, pieces[2 * pad:2 * pad + heads], (0, 0))

    for distance in range(1, head_devices):

        @pl.when(my_head + distance < head_devices)
        def _():
            pl.semaphore_wait(head_ready.at[distance - 1], 1)

    for away in range(1, members):
        remote(
            gw_slots.at[flat], gw_slots.at[flat], gw_send, gw_recv,
            **member(lax.rem(flat + away, members)),
        ).start()
    for away in range(1, head_devices):
        remote(
            lat_slots.at[my_head], lat_slots.at[my_head], lat_send, lat_recv,
            head=lax.rem(my_head + away, head_devices),
        ).start()

    finish_heads()
    passed = t_ref.at[pl.ds(0, layer - 1)]
    remote(passed, passed, t_send, t_recv.at[0], seq=mate).wait_send()
    remote(mate_in, mate_in, mate_send, mate_recv.at[0], seq=mate).wait_send()
    passed = rs_out.at[pl.ds(0, CHIPS - 1)]
    remote(passed, passed, rs_send, rs_recv.at[0], seq=mate).wait_send()
    passed = ag_out.at[pl.ds(0, CHIPS - 1)]
    remote(passed, passed, ag_send, ag_recv.at[0], seq=mate).wait_send()
    remote(back_out, back_out, back_send, back_recv, seq=mate).wait_send()
    for distance in range(1, blocks):
        pl.when(sends_to(distance))(
            remote(
                blk_out, blk_out, blk_send.at[distance - 1], blk_recv.at[0, 0], seq=mate
            ).wait_send
        )
    peer = {"head": lax.rem(my_head + 1, head_devices)}
    if head_devices > 1:
        passed = lat_slots.at[pl.ds(0, head_devices - 1)]
        lats = remote(passed, passed, lat_send, lat_recv, **peer)
        lats.wait_recv()
    total = lat_slots[0]
    for slot in range(1, head_devices):
        total = total + lat_slots[slot]
    glat_ref[...] = total
    passed = gw_slots.at[pl.ds(0, members - 1)]
    sums = remote(passed, passed, gw_send, gw_recv, seq=mate)
    sums.wait_recv()
    total = gw_slots[0]
    for slot in range(1, members):
        total = total + gw_slots[slot]
    gw_ref[...] = total

    if head_devices > 1:
        lats.wait_send()
    sums.wait_send()


def emit_kernel(gq, gk, gv, glat, gw, oq, ok, ov, olat, ow):
    oq[...] = gq[...]
    ok[...] = gk[...]
    ov[...] = gv[...]
    olat[...] = glat[...]
    for head in range(ow.shape[0]):
        ow[head:head + 1] = gw[:, head * ow.shape[1]:(head + 1) * ow.shape[1]]


def emit(results, rows, width, rank, heads):
    vmem = pl.BlockSpec(memory_space=pltpu.VMEM)
    hbm = pl.BlockSpec(memory_space=pl.ANY)
    wide = jax.ShapeDtypeStruct((rows, width), BF16)
    return pl.pallas_call(
        emit_kernel,
        out_shape=(
            wide, wide, wide,
            jax.ShapeDtypeStruct((rank, rows), F32), jax.ShapeDtypeStruct((heads, rank), F32),
        ),
        in_specs=[vmem] * 5,
        out_specs=(vmem,) * 5,

        name="emit",
    )(*(pltpu.with_memory_space_constraint(result, pltpu.VMEM) for result in results))


def on_device(sizes, *args):
    queries, keys_in, values, grad_out, latent, gate_weight, gate_bias, doc_starts, block_docs = args
    rows, width = queries.shape[1], queries.shape[2]
    rank = latent.shape[2]
    seq_count, dp_count, head_devices = sizes
    heads = width // HEAD_DIM
    quarter = heads // CHIPS
    layer = PAIR * CHIPS
    far = max(1, seq_count // layer - 1)
    members = seq_count * dp_count
    pad = -(-heads // 8) * 8
    square = lambda *lead: pltpu.VMEM((*lead, HEAD_DIM, HEAD_DIM), F32)
    dma = lambda *shape: pltpu.SemaphoreType.DMA(shape)
    single = pltpu.SemaphoreType.DMA
    hbm = pl.BlockSpec(memory_space=pltpu.HBM)
    wide = pltpu.VMEM((rows, width), BF16)
    results = pl.pallas_call(
        functools.partial(kernel, (seq_count, dp_count, head_devices, heads)),
        out_shape=(
            wide, wide, wide, pltpu.VMEM((rank, rows), F32), pltpu.VMEM((1, LANES), F32),
        ),
        in_specs=[hbm] * 8,
        scratch_shapes=[
            pltpu.VMEM((4, rows, width), BF16),
            pltpu.VMEM((rank, rows), BF16),
            pltpu.VMEM((heads, rank), BF16),
            pltpu.VMEM((1, heads), F32),
            pltpu.VMEM(doc_starts.shape, jnp.int32),
            pltpu.VMEM((LANES, rows), BF16),
            pltpu.VMEM((3 * pad, rows), F32),
            pltpu.VMEM((LANES, rows), F32),
            pltpu.VMEM((rows, LANES), F32),
            pltpu.VMEM((rows, rows), BF16),
            pltpu.VMEM((rows, width), F32),
            pltpu.VMEM((rows, width), F32),
            pltpu.VMEM((rows, width), F32),
            pltpu.VMEM((2, heads, HEAD_DIM, rows), BF16),
            pltpu.VMEM((heads, HEAD_DIM, rows), BF16),
            pltpu.VMEM((pad, rows), F32),
            pltpu.VMEM((2 * pad, rows), F32),
            pltpu.VMEM((layer, 8, LANES), F32),
            square(2, heads), square(heads), square(CHIPS, quarter), square(CHIPS, quarter),
            pltpu.VMEM((quarter, LEAD + HEAD_DIM, HEAD_DIM), F32),
            pltpu.VMEM((far, quarter, LEAD + HEAD_DIM, HEAD_DIM), F32),
            square(CHIPS, quarter), square(heads), square(2, heads),
            pltpu.VMEM((head_devices, rank, rows), F32),
            pltpu.VMEM((members, 1, LANES), F32),
            dma(4), dma(4), single, dma(2), single, dma(heads), single, dma(CHUNKS),
            dma(far), dma(far, CHUNKS), single, dma(CHIPS), single, single,
            single, single, single, single,
            pltpu.SemaphoreType.REGULAR((far,)),
            pltpu.SemaphoreType.REGULAR((max(1, head_devices - 1),)),
        ],
        compiler_params=pltpu.CompilerParams(collective_id=0, has_side_effects=True),
        name="gated_backward",
    )(
        keys_in[0], queries[0], values[0], grad_out[0], latent[0].T, gate_weight.T,
        gate_bias[None, :], doc_starts,
    )
    out = emit(results, rows, width, rank, heads)
    return out[0][None], out[1][None], out[2][None], out[3].T[None], out[4].T


def solution(mesh):
    sizes = (mesh.shape["seq"], mesh.shape["dp"], mesh.shape["head"])
    return jax.shard_map(
        functools.partial(on_device, sizes),
        mesh=mesh,
        in_specs=(
            P(("groups", "dp"), "seq", "head"),
            P(("groups", "dp"), "seq", "head"),
            P(("groups", "dp"), "seq", "head"),
            P(("groups", "dp"), "seq", "head"),
            P(("groups", "dp"), "seq", None),
            P(None, "head"),
            P("head"),
            P(("groups", "dp"), None),
            P(("groups", "dp"), "seq"),
        ),
        out_specs=(
            P(("groups", "dp"), "seq", "head"),
            P(("groups", "dp"), "seq", "head"),
            P(("groups", "dp"), "seq", "head"),
            P(("groups", "dp"), "seq", None),
            P("groups", "head"),
        ),
        check_vma=False,
    )
```

```python
import functools
import math

import jax
import jax.numpy as jnp
from jax import lax
from jax.experimental import pallas as pl
from jax.experimental.pallas import tpu as pltpu
from jax.sharding import PartitionSpec as P

HEAD_DIM = 128
LANES = 128
PAIR = 2
CHIPS = 4
LEAD = 8
CHUNKS = 4
PIECE = HEAD_DIM // CHUNKS

MESH = pl.DeviceIdType.MESH
F32 = jnp.float32
BF16 = jnp.bfloat16


def dot(left, right, over):
    return lax.dot_general(
        left, right, (((over[0],), (over[1],)), ((), ())), preferred_element_type=F32,
    )


def halves(tensor):
    upper = tensor.astype(BF16)
    return upper, (tensor - upper.astype(F32)).astype(BF16)


def thirds(tensor):
    upper, rest = tensor.astype(BF16), None
    rest = tensor - upper.astype(F32)
    middle = rest.astype(BF16)
    return upper.astype(F32), middle.astype(F32), rest - middle.astype(F32)


def kernel(
    sizes,
    k_hbm, q_hbm, v_hbm, g_hbm, latent_hbm, weight_hbm, bias_hbm, bounds_hbm,
    gq_ref, gk_ref, gv_ref, glat_ref, gw_ref,
    x_ref, latent_ref, weight_ref, bias_ref, bounds_ref,
    tiled_ref, stack_ref, rows_ref, cols_ref, upto_ref, iq_ref, ik_ref, iv_ref, left_ref, value_ref, base_ref, through_ref,
    t_ref, part_ref, mate_in, rs_out, rs_in, blk_out, blk_in, ag_out, back_out, state_ref,
    lat_slots, gw_slots,
    load_sem, small_sem, t_send, t_recv, mate_send, mate_recv, rs_send, rs_recv,
    blk_send, blk_recv, ag_send, ag_recv, back_send, back_recv,
    lat_send, lat_recv, gw_send, gw_recv, block_ready, head_ready,
):
    seq_count, dp_count, head_devices, heads = sizes
    rows = x_ref.shape[1]
    quarter = heads // CHIPS
    layer = PAIR * CHIPS
    blocks = seq_count // layer
    rank = latent_ref.shape[0]
    pad = stack_ref.shape[0] // 3
    scaling = 1.0 / math.sqrt(HEAD_DIM)
    me = lax.axis_index("seq")
    my_dp = lax.axis_index("dp")
    my_head = lax.axis_index("head")
    core = lax.rem(me, PAIR)
    chip = lax.rem(lax.div(me, PAIR), CHIPS)
    block = lax.div(me, layer)
    group = block * layer
    place = core + PAIR * chip
    mate = me + 1 - 2 * core
    members = seq_count * dp_count
    flat = me * dp_count + my_dp
    beside = chip + 1 - 2 * lax.rem(chip, 2)
    above = chip + 2 - 4 * lax.div(chip, 2)
    opposite = CHIPS - 1 - chip
    others = (opposite, above, beside)

    def at_chip(index):
        return group + index * PAIR + core

    def at_block(distance):
        return me + jnp.where(core == 0, distance, -distance) * layer

    def sends_to(distance):
        return jnp.where(core == 0, block + distance < blocks, block >= distance)

    def hears_from(distance):
        return jnp.where(core == 0, block >= distance, block + distance < blocks)

    def member(index):
        return {"seq": lax.div(index, dp_count), "dp": lax.rem(index, dp_count)}

    def greet(semaphore, **where):
        pl.semaphore_signal(semaphore, inc=1, device_id=where, device_id_type=MESH)

    small = [
        pltpu.make_async_copy(source, target, small_sem.at[index])
        for index, (source, target) in enumerate((
            (latent_hbm, latent_ref), (weight_hbm, weight_ref),
            (bias_hbm, bias_ref), (bounds_hbm, bounds_ref),
        ))
    ]
    loads = [
        pltpu.make_async_copy(source, x_ref.at[index], load_sem.at[index])
        for index, source in enumerate((k_hbm, q_hbm, v_hbm, g_hbm))
    ]
    for copy in small:
        copy.start()

    barrier = pltpu.get_barrier_semaphore()
    greeted = layer - 1 + seq_count * (dp_count - 1)
    for away in range(1, layer):
        greet(barrier, seq=group + lax.rem(place + away, layer))
    for away in range(1, dp_count):
        for there in range(seq_count):
            greet(barrier, seq=there, dp=lax.rem(my_dp + away, dp_count))
    for distance in range(1, blocks):

        @pl.when(block + distance < blocks)
        def _():
            greet(barrier, seq=me + distance * layer)

        greeted = greeted + jnp.where(block >= distance, 1, 0)
    for distance in range(1, head_devices):

        @pl.when(my_head + distance < head_devices)
        def _():
            greet(barrier, head=my_head + distance)

        greeted = greeted + jnp.where(my_head >= distance, 1, 0)

    @pl.when(core == 0)
    def _():
        for index in (1, 3, 0, 2):
            loads[index].start()

    @pl.when(core == 1)
    def _():
        for index in (0, 2, 1, 3):
            loads[index].start()

    row_id = lax.broadcasted_iota(jnp.int32, (rows, rows), 0)
    col_id = lax.broadcasted_iota(jnp.int32, (rows, rows), 1)
    upto_ref[...] = (row_id <= col_id).astype(F32).astype(BF16)
    stack_ref[...] = jnp.zeros_like(stack_ref)
    rows_ref[...] = jnp.zeros_like(rows_ref)

    def stacked(tensor):
        for index, piece in enumerate(thirds(tensor)):
            stack_ref[index * pad:index * pad + heads] = piece
        return stack_ref[...].astype(BF16)

    def unstacked(tensor):
        return (tensor[0:heads] + tensor[pad:pad + heads]) + tensor[2 * pad:2 * pad + heads]

    for copy in small:
        copy.wait()
    gate_rows = dot(weight_ref[...], latent_ref[...], (1, 0))
    eye = lax.broadcasted_iota(jnp.int32, (heads, heads), 0) == lax.broadcasted_iota(
        jnp.int32, (heads, heads), 1
    )
    bias = jnp.sum(jnp.where(eye, bias_ref[...], 0.0), axis=1, keepdims=True)
    gate_rows = gate_rows + bias
    log_decay = (jnp.minimum(gate_rows, 0.0) - jnp.log1p(jnp.exp(-jnp.abs(gate_rows)))) / 16.0
    cumul = unstacked(dot(stacked(log_decay), upto_ref[...], (1, 0)))
    first_pos = me * rows
    bounds = bounds_ref[...]
    position = first_pos + lax.broadcasted_iota(jnp.int32, (rows, bounds.shape[1]), 0)
    opened = jnp.where((bounds >= first_pos) & (bounds <= position), 1.0, 0.0).astype(BF16)
    docs = dot(jnp.ones((8, bounds.shape[1]), BF16), opened, (1, 1))
    doc_row = docs[0:1]
    doc_last = doc_row[:, rows - 1:]
    ending = cumul[:, rows - 1:]
    through = jnp.where(doc_last == 0.0, jnp.exp(ending), 0.0)
    rows_ref[0:heads] = jnp.where(doc_row == doc_last, jnp.exp(ending - cumul), 0.0)
    rows_ref[heads:2 * heads] = jnp.where(doc_row == 0.0, jnp.exp(cumul), 0.0) * scaling
    rows_ref[2 * heads:3 * heads] = cumul
    rows_ref[3 * heads:3 * heads + 8] = docs
    through_ref[2 * pad:2 * pad + heads] = (1.0 / (1.0 + jnp.exp(gate_rows))) / 16.0
    t_ref[place, 0:heads] = jnp.broadcast_to(through, (heads, LANES))

    def column(index):
        return cols_ref[:, index:index + 1]

    def head_lanes(index):
        return pl.ds(index * HEAD_DIM, HEAD_DIM)

    def remote(source, target, send_sem, recv_sem, **where):
        return pltpu.make_async_remote_copy(
            src_ref=source, dst_ref=target, send_sem=send_sem, recv_sem=recv_sem,
            device_id=where, device_id_type=MESH,
        )

    pl.semaphore_wait(barrier, greeted)
    for distance in range(1, blocks):

        @pl.when(block >= distance)
        def _():
            greet(block_ready.at[distance - 1], seq=me - distance * layer)

    for distance in range(1, head_devices):

        @pl.when(my_head >= distance)
        def _():
            greet(head_ready.at[distance - 1], head=my_head - distance)


    def decay_copy(target, slot):
        return remote(
            t_ref.at[slot], t_ref.at[slot], t_send,
            t_recv.at[0 if target is mate else 1], seq=target,
        )

    decay_copy(mate, place).start()

    def mate_copy(head):
        return remote(
            part_ref.at[1 - core, head], mate_in.at[head], mate_send, mate_recv.at[head], seq=mate
        )

    def span(c):
        return pl.ds(c * PIECE, PIECE)

    def block_span(c):
        return pl.ds(0, LEAD + PIECE) if c == 0 else pl.ds(LEAD + c * PIECE, PIECE)

    def rs_copy(target, source, i, c):
        return remote(
            rs_out.at[target, i, span(c)], rs_in.at[source, i, span(c)],
            rs_send, rs_recv.at[c], seq=at_chip(target),
        )

    def blk_copy(distance, i, c):
        return remote(
            blk_out.at[i, block_span(c)], blk_in.at[distance - 1, i, block_span(c)],
            blk_send.at[distance - 1], blk_recv.at[distance - 1, c], seq=at_block(distance),
        )

    def ag_copy(target, source, i, c):
        return remote(
            ag_out.at[target, i, span(c)], state_ref.at[core, source * quarter + i, span(c)],
            ag_send, ag_recv.at[source], seq=at_chip(target),
        )

    def back_copy(head):
        return remote(
            back_out.at[head], state_ref.at[core, head], back_send, back_recv, seq=mate
        )

    order = [(whose, i) for whose in (*others, chip) for i in range(quarter)]

    def part(way, head):
        lanes = pl.ds(pl.multiple_of(head * HEAD_DIM, HEAD_DIM), HEAD_DIM)
        turned = x_ref[way, :, lanes].T
        left_ref[way, head] = turned
        upper, lower = halves(turned.astype(F32) * rows_ref[pl.ds(way * heads + head, 1)])
        right = x_ref[2 + way, :, lanes]
        part_ref[way, head] = dot(upper, right, (1, 0)) + dot(lower, right, (1, 0))

    def load_wait(way):
        for index in (way, 2 + way):
            pltpu.make_async_copy(k_hbm, x_ref.at[index], load_sem.at[index]).wait()

    load_wait(1 - core)
    for first in range(0, heads, 4):
        batch = [whose * quarter + i for whose, i in order[first:first + 4]]
        for head in batch:
            part(1 - core, head)
        for head in batch:
            mate_copy(head).start()
    for whose in others:
        for peer in range(PAIR):
            decay_copy(group + whose * PAIR + peer, place).start()
    load_wait(core)
    for whose, i in order:
        part(core, whose * quarter + i)

    decay_copy(mate, place).wait_recv()

    def decay_of(index, head):
        return t_ref[index, pl.ds(head, 1), :]

    def send_parts():
        for whose, i in order:
            head = whose * quarter + i
            keep = decay_of(PAIR * chip + 1 - core, head)
            mate_copy(head).wait_recv()
            total = keep * part_ref[core, head] + mate_in[head]
            if whose is chip:
                rs_in[chip, i] = total
            else:
                rs_out[whose, i] = total
                for c in range(CHUNKS // 2):
                    rs_copy(whose, chip, i, c).start()
        for whose, i in order:
            if whose is not chip:
                for c in range(CHUNKS // 2, CHUNKS):
                    rs_copy(whose, chip, i, c).start()

    lane_id = lax.broadcasted_iota(jnp.int32, (rows, LANES), 1)

    def local_head(head):
        lanes = head_lanes(head)
        key, query, value, grad = (x_ref[index, :, lanes] for index in range(4))
        same_doc = (row_id >= col_id) & (column(3 * heads) == rows_ref[3 * heads:3 * heads + 1])
        spread = jnp.where(
            same_doc, column(2 * heads + head) - rows_ref[2 * heads + head:2 * heads + head + 1], 0.0
        )
        weights = jnp.where(same_doc, jnp.exp(spread), 0.0)
        scores = dot(query, key, (1, 1)) * scaling * weights
        pair_dots = dot(grad, value, (1, 1))
        weighted = (pair_dots * weights * scaling).astype(BF16)
        products = scores * pair_dots
        iv_ref[:, lanes] = dot(scores.astype(BF16), grad, (0, 0))
        iq_ref[:, lanes] = dot(weighted, key, (1, 0))
        ik_ref[:, lanes] = dot(weighted, query, (0, 0))
        flows.append(jnp.sum(products, axis=1, keepdims=True))
        base_ref[head:head + 1] = jnp.sum(products, axis=0, keepdims=True)

    passes_on = sends_to(1)
    pl.when(passes_on)(send_parts)
    for index in range(LANES // rank):
        tiled_ref[index * rank:(index + 1) * rank] = latent_ref[...]
    cols_ref[...] = rows_ref[...].T
    flows = []
    for head in range(heads):
        local_head(head)
    pl.when(jnp.logical_not(passes_on))(send_parts)
    gathered = jnp.zeros((rows, LANES), F32)
    for head in range(heads):
        gathered = jnp.where(lane_id == head, flows[head], gathered)
        value_ref[head] = x_ref[2, :, head_lanes(head)].T
    base_ref[0:heads] = gathered.T[0:heads] - base_ref[0:heads]

    def kth(k):
        return jnp.where(core == 0, k, CHIPS - 1 - k)

    def chip_decay(index, head):
        return decay_of(PAIR * index, head) * decay_of(PAIR * index + 1, head)

    passed = t_ref.at[pl.ds(0, layer - PAIR)]
    remote(passed, passed, t_send, t_recv.at[1], seq=mate).wait_recv()
    for distance in range(1, blocks):

        @pl.when(block + distance < blocks)
        def _():
            pl.semaphore_wait(block_ready.at[distance - 1], 1)

    for c in range(CHUNKS):
        passed = rs_in.at[pl.ds(0, CHIPS - 1), :, span(c)]
        remote(passed, passed, rs_send, rs_recv.at[c], seq=mate).wait_recv()
        for i in range(quarter):
            head = chip * quarter + i
            total = rs_in[kth(0), i, span(c)]
            for k in range(1, CHIPS):
                total = chip_decay(kth(k), head) * total + rs_in[kth(k), i, span(c)]
            blk_out[i, pl.ds(LEAD + c * PIECE, PIECE)] = total
            if c == 0:
                across = chip_decay(0, head)
                for k in range(1, CHIPS):
                    across = across * chip_decay(k, head)
                blk_out[i, 0:LEAD] = jnp.broadcast_to(across, (LEAD, LANES))
            for distance in range(1, blocks):
                pl.when(sends_to(distance))(blk_copy(distance, i, c).start)

    for c in range(CHUNKS):
        for i in range(quarter):
            entering = jnp.zeros((PIECE, HEAD_DIM), F32)
            for distance in range(blocks - 1, 0, -1):
                hears = hears_from(distance)
                pl.when(hears)(blk_copy(distance, i, c).wait_recv)

                @pl.when(jnp.logical_not(hears))
                def _():
                    blk_in[distance - 1, i, block_span(c)] = jnp.zeros(
                        (PIECE + (LEAD if c == 0 else 0), HEAD_DIM), F32
                    )

                entering = (
                    blk_in[distance - 1, i, 0:1] * entering
                    + blk_in[distance - 1, i, pl.ds(LEAD + c * PIECE, PIECE)]
                )
            head = chip * quarter + i
            for k in range(CHIPS):
                ag_out[kth(k), i, span(c)] = entering
                if k < CHIPS - 1:
                    entering = chip_decay(kth(k), head) * entering + rs_in[kth(k), i, span(c)]
            for target in others:
                ag_copy(target, chip, i, c).start()

    for whose in (chip, beside, above, opposite):
        mine = pl.ds(whose * quarter, quarter)
        if whose is not chip:
            remote(
                ag_out.at[whose], state_ref.at[core, mine], ag_send, ag_recv.at[whose], seq=mate
            ).wait_recv()
        for i in range(quarter):
            head = whose * quarter + i
            if whose is chip:
                state_ref[core, head] = ag_out[chip, i]
            back_out[head] = decay_of(place, head) * state_ref[core, head] + part_ref[core, head]
            back_copy(head).start()

    def state_rows():
        for head in range(heads):
            upper, lower = halves(state_ref[0, head])
            grad = x_ref[3, :, head_lanes(head)]
            carried = dot(upper, grad, (1, 1)) + dot(lower, grad, (1, 1))
            inflow = jnp.sum(carried * left_ref[1, head].astype(F32), axis=0, keepdims=True)
            through_ref[head:head + 1] = inflow * rows_ref[heads + head:heads + head + 1]

    def back_rows():
        for head in range(heads):
            upper, lower = halves(state_ref[1, head])
            key = x_ref[0, :, head_lanes(head)]
            carried = dot(upper, key, (0, 1)) + dot(lower, key, (0, 1))
            outflow = jnp.sum(carried * value_ref[head].astype(F32), axis=0, keepdims=True)
            through_ref[pad + head:pad + head + 1] = outflow * rows_ref[head:head + 1]

    def finish_heads():
        for head in range(heads):
            lanes = head_lanes(head)
            key, query, value, grad = (x_ref[index, :, lanes] for index in range(4))
            enter, leave = column(heads + head), column(head)
            upper, lower = halves(state_ref[0, head])
            carried = (dot(grad, upper, (1, 1)) + dot(grad, lower, (1, 1))) * enter
            gq_ref[:, lanes] = (iq_ref[:, lanes] + carried).astype(BF16)
            upper, lower = halves(state_ref[1, head])
            carried = (dot(key, upper, (1, 0)) + dot(key, lower, (1, 0))) * leave
            gv_ref[:, lanes] = (iv_ref[:, lanes] + carried).astype(BF16)
            carried = dot(value, upper, (1, 1)) * leave
            gk_ref[:, lanes] = (ik_ref[:, lanes] + carried).astype(BF16)

    pl.when(core == 0)(state_rows)
    pl.when(core == 1)(back_rows)
    remote(back_out, state_ref.at[1 - core], back_send, back_recv, seq=mate).wait_recv()
    pl.when(core == 0)(back_rows)
    pl.when(core == 1)(state_rows)

    wholes = [
        jnp.sum(jnp.sum(state_ref[0, head] * state_ref[1, head], axis=0, keepdims=True), axis=1, keepdims=True)
        for head in range(heads)
    ]
    inflow, outflow = through_ref[0:heads], through_ref[pad:pad + heads]
    end_term = through * jnp.concatenate(wholes, axis=0) + jnp.sum(outflow, axis=1, keepdims=True)
    row_lane = lax.broadcasted_iota(jnp.int32, (heads, rows), 1)
    grad_cumul = base_ref[0:heads] + (inflow - outflow) + jnp.where(
        row_lane == rows - 1, end_term, 0.0
    )
    grad_log = unstacked(dot(stacked(grad_cumul), upto_ref[...], (1, 1)))
    grad_gate = grad_log * through_ref[2 * pad:2 * pad + heads]
    pieces = stacked(grad_gate)
    spread = unstacked(dot(pieces, tiled_ref[...], (1, 1)))
    lane = lax.broadcasted_iota(jnp.int32, (heads, LANES), 1)
    owner = lax.broadcasted_iota(jnp.int32, (heads, LANES), 0)
    gw_slots[flat] = jnp.sum(
        jnp.where(lax.div(lane, rank) == owner, spread, 0.0), axis=0, keepdims=True
    )
    for away in range(1, members):
        remote(
            gw_slots.at[flat], gw_slots.at[flat], gw_send, gw_recv,
            **member(lax.rem(flat + away, members)),
        ).start()
    weight = weight_ref[...]
    lat_slots[my_head] = (
        dot(weight, pieces[0:heads], (0, 0)) + dot(weight, pieces[pad:pad + heads], (0, 0))
    ) + dot(weight, pieces[2 * pad:2 * pad + heads], (0, 0))

    for distance in range(1, head_devices):

        @pl.when(my_head + distance < head_devices)
        def _():
            pl.semaphore_wait(head_ready.at[distance - 1], 1)

    for away in range(1, head_devices):
        remote(
            lat_slots.at[my_head], lat_slots.at[my_head], lat_send, lat_recv,
            head=lax.rem(my_head + away, head_devices),
        ).start()

    finish_heads()
    passed = t_ref.at[pl.ds(0, layer - 1)]
    remote(passed, passed, t_send, t_recv.at[0], seq=mate).wait_send()
    remote(mate_in, mate_in, mate_send, mate_recv.at[0], seq=mate).wait_send()
    passed = rs_out.at[pl.ds(0, CHIPS - 1)]
    remote(passed, passed, rs_send, rs_recv.at[0], seq=mate).wait_send()
    passed = ag_out.at[pl.ds(0, CHIPS - 1)]
    remote(passed, passed, ag_send, ag_recv.at[0], seq=mate).wait_send()
    remote(back_out, back_out, back_send, back_recv, seq=mate).wait_send()
    for distance in range(1, blocks):
        pl.when(sends_to(distance))(
            remote(
                blk_out, blk_out, blk_send.at[distance - 1], blk_recv.at[0, 0], seq=mate
            ).wait_send
        )
    peer = {"head": lax.rem(my_head + 1, head_devices)}
    if head_devices > 1:
        passed = lat_slots.at[pl.ds(0, head_devices - 1)]
        lats = remote(passed, passed, lat_send, lat_recv, **peer)
        lats.wait_recv()
    total = lat_slots[0]
    for slot in range(1, head_devices):
        total = total + lat_slots[slot]
    glat_ref[...] = total
    passed = gw_slots.at[pl.ds(0, members - 1)]
    sums = remote(passed, passed, gw_send, gw_recv, seq=mate)
    sums.wait_recv()
    total = gw_slots[0]
    for slot in range(1, members):
        total = total + gw_slots[slot]
    gw_ref[...] = total

    if head_devices > 1:
        lats.wait_send()
    sums.wait_send()


def emit_kernel(gq, gk, gv, glat, gw, oq, ok, ov, olat, ow):
    oq[...] = gq[...]
    ok[...] = gk[...]
    ov[...] = gv[...]
    olat[...] = glat[...]
    for head in range(ow.shape[0]):
        ow[head:head + 1] = gw[:, head * ow.shape[1]:(head + 1) * ow.shape[1]]


def emit(results, rows, width, rank, heads):
    vmem = pl.BlockSpec(memory_space=pltpu.VMEM)
    hbm = pl.BlockSpec(memory_space=pl.ANY)
    wide = jax.ShapeDtypeStruct((rows, width), BF16)
    return pl.pallas_call(
        emit_kernel,
        out_shape=(
            wide, wide, wide,
            jax.ShapeDtypeStruct((rank, rows), F32), jax.ShapeDtypeStruct((heads, rank), F32),
        ),
        in_specs=[vmem] * 5,
        out_specs=(vmem,) * 5,

        name="emit",
    )(*(pltpu.with_memory_space_constraint(result, pltpu.VMEM) for result in results))


def on_device(sizes, *args):
    queries, keys_in, values, grad_out, latent, gate_weight, gate_bias, doc_starts, block_docs = args
    rows, width = queries.shape[1], queries.shape[2]
    rank = latent.shape[2]
    seq_count, dp_count, head_devices = sizes
    heads = width // HEAD_DIM
    quarter = heads // CHIPS
    layer = PAIR * CHIPS
    far = max(1, seq_count // layer - 1)
    members = seq_count * dp_count
    pad = -(-heads // 8) * 8
    square = lambda *lead: pltpu.VMEM((*lead, HEAD_DIM, HEAD_DIM), F32)
    dma = lambda *shape: pltpu.SemaphoreType.DMA(shape)
    single = pltpu.SemaphoreType.DMA
    hbm = pl.BlockSpec(memory_space=pltpu.HBM)
    wide = pltpu.VMEM((rows, width), BF16)
    results = pl.pallas_call(
        functools.partial(kernel, (seq_count, dp_count, head_devices, heads)),
        out_shape=(
            wide, wide, wide, pltpu.VMEM((rank, rows), F32), pltpu.VMEM((1, LANES), F32),
        ),
        in_specs=[hbm] * 8,
        scratch_shapes=[
            pltpu.VMEM((4, rows, width), BF16),
            pltpu.VMEM((rank, rows), BF16),
            pltpu.VMEM((heads, rank), BF16),
            pltpu.VMEM((1, heads), F32),
            pltpu.VMEM(doc_starts.shape, jnp.int32),
            pltpu.VMEM((LANES, rows), BF16),
            pltpu.VMEM((3 * pad, rows), F32),
            pltpu.VMEM((LANES, rows), F32),
            pltpu.VMEM((rows, LANES), F32),
            pltpu.VMEM((rows, rows), BF16),
            pltpu.VMEM((rows, width), F32),
            pltpu.VMEM((rows, width), F32),
            pltpu.VMEM((rows, width), F32),
            pltpu.VMEM((2, heads, HEAD_DIM, rows), BF16),
            pltpu.VMEM((heads, HEAD_DIM, rows), BF16),
            pltpu.VMEM((pad, rows), F32),
            pltpu.VMEM((3 * pad, rows), F32),
            pltpu.VMEM((layer, 8, LANES), F32),
            square(2, heads), square(heads), square(CHIPS, quarter), square(CHIPS, quarter),
            pltpu.VMEM((quarter, LEAD + HEAD_DIM, HEAD_DIM), F32),
            pltpu.VMEM((far, quarter, LEAD + HEAD_DIM, HEAD_DIM), F32),
            square(CHIPS, quarter), square(heads), square(2, heads),
            pltpu.VMEM((head_devices, rank, rows), F32),
            pltpu.VMEM((members, 1, LANES), F32),
            dma(4), dma(4), single, dma(2), single, dma(heads), single, dma(CHUNKS),
            dma(far), dma(far, CHUNKS), single, dma(CHIPS), single, single,
            single, single, single, single,
            pltpu.SemaphoreType.REGULAR((far,)),
            pltpu.SemaphoreType.REGULAR((max(1, head_devices - 1),)),
        ],
        compiler_params=pltpu.CompilerParams(collective_id=0, has_side_effects=True),
        name="gated_backward",
    )(
        keys_in[0], queries[0], values[0], grad_out[0], latent[0].T, gate_weight.T,
        gate_bias[None, :], doc_starts,
    )
    out = emit(results, rows, width, rank, heads)
    return out[0][None], out[1][None], out[2][None], out[3].T[None], out[4].T


def solution(mesh):
    sizes = (mesh.shape["seq"], mesh.shape["dp"], mesh.shape["head"])
    return jax.shard_map(
        functools.partial(on_device, sizes),
        mesh=mesh,
        in_specs=(
            P(("groups", "dp"), "seq", "head"),
            P(("groups", "dp"), "seq", "head"),
            P(("groups", "dp"), "seq", "head"),
            P(("groups", "dp"), "seq", "head"),
            P(("groups", "dp"), "seq", None),
            P(None, "head"),
            P("head"),
            P(("groups", "dp"), None),
            P(("groups", "dp"), "seq"),
        ),
        out_specs=(
            P(("groups", "dp"), "seq", "head"),
            P(("groups", "dp"), "seq", "head"),
            P(("groups", "dp"), "seq", "head"),
            P(("groups", "dp"), "seq", None),
            P("groups", "head"),
        ),
        check_vma=False,
    )
```

```python
import functools
import math

import jax
import jax.numpy as jnp
from jax import lax
from jax.experimental import pallas as pl
from jax.experimental.pallas import tpu as pltpu
from jax.sharding import PartitionSpec as P

HEAD_DIM = 128
LANES = 128
PAIR = 2
CHIPS = 4
LEAD = 8
CHUNKS = 4
PIECE = HEAD_DIM // CHUNKS

MESH = pl.DeviceIdType.MESH
F32 = jnp.float32
BF16 = jnp.bfloat16


def dot(left, right, over):
    return lax.dot_general(
        left, right, (((over[0],), (over[1],)), ((), ())), preferred_element_type=F32,
    )


def halves(tensor):
    upper = tensor.astype(BF16)
    return upper, (tensor - upper.astype(F32)).astype(BF16)


def thirds(tensor):
    upper, rest = tensor.astype(BF16), None
    rest = tensor - upper.astype(F32)
    middle = rest.astype(BF16)
    return upper.astype(F32), middle.astype(F32), rest - middle.astype(F32)


def kernel(
    sizes,
    k_hbm, q_hbm, v_hbm, g_hbm, latent_hbm, weight_hbm, bias_hbm, bounds_hbm,
    gq_ref, gk_ref, gv_ref, glat_ref, gw_ref,
    x_ref, latent_ref, weight_ref, bias_ref, bounds_ref,
    tiled_ref, stack_ref, rows_ref, cols_ref, upto_ref, iq_ref, ik_ref, iv_ref, left_ref, value_ref, base_ref, through_ref,
    t_ref, part_ref, mate_in, rs_out, rs_in, blk_out, blk_in, ag_out, back_out, state_ref,
    lat_slots, gw_slots,
    load_sem, small_sem, t_send, t_recv, mate_send, mate_recv, rs_send, rs_recv,
    blk_send, blk_recv, ag_send, ag_recv, back_send, back_recv,
    lat_send, lat_recv, gw_send, gw_recv, block_ready, head_ready,
):
    seq_count, dp_count, head_devices, heads = sizes
    rows = x_ref.shape[1]
    quarter = heads // CHIPS
    layer = PAIR * CHIPS
    blocks = seq_count // layer
    rank = latent_ref.shape[0]
    pad = stack_ref.shape[0] // 3
    scaling = 1.0 / math.sqrt(HEAD_DIM)
    me = lax.axis_index("seq")
    my_dp = lax.axis_index("dp")
    my_head = lax.axis_index("head")
    core = lax.rem(me, PAIR)
    chip = lax.rem(lax.div(me, PAIR), CHIPS)
    block = lax.div(me, layer)
    group = block * layer
    place = core + PAIR * chip
    mate = me + 1 - 2 * core
    members = seq_count * dp_count
    flat = me * dp_count + my_dp
    beside = chip + 1 - 2 * lax.rem(chip, 2)
    above = chip + 2 - 4 * lax.div(chip, 2)
    opposite = CHIPS - 1 - chip
    others = (opposite, above, beside)

    def at_chip(index):
        return group + index * PAIR + core

    def at_block(distance):
        return me + jnp.where(core == 0, distance, -distance) * layer

    def sends_to(distance):
        return jnp.where(core == 0, block + distance < blocks, block >= distance)

    def hears_from(distance):
        return jnp.where(core == 0, block >= distance, block + distance < blocks)

    def member(index):
        return {"seq": lax.div(index, dp_count), "dp": lax.rem(index, dp_count)}

    def greet(semaphore, **where):
        pl.semaphore_signal(semaphore, inc=1, device_id=where, device_id_type=MESH)

    small = [
        pltpu.make_async_copy(source, target, small_sem.at[index])
        for index, (source, target) in enumerate((
            (latent_hbm, latent_ref), (weight_hbm, weight_ref),
            (bias_hbm, bias_ref), (bounds_hbm, bounds_ref),
        ))
    ]
    loads = [
        pltpu.make_async_copy(source, x_ref.at[index], load_sem.at[index])
        for index, source in enumerate((k_hbm, q_hbm, v_hbm, g_hbm))
    ]
    for copy in small:
        copy.start()

    barrier = pltpu.get_barrier_semaphore()
    greeted = layer - 1 + seq_count * (dp_count - 1)
    for away in range(1, layer):
        greet(barrier, seq=group + lax.rem(place + away, layer))
    for away in range(1, dp_count):
        for there in range(seq_count):
            greet(barrier, seq=there, dp=lax.rem(my_dp + away, dp_count))
    for distance in range(1, blocks):

        @pl.when(block + distance < blocks)
        def _():
            greet(barrier, seq=me + distance * layer)

        greeted = greeted + jnp.where(block >= distance, 1, 0)
    for distance in range(1, head_devices):

        @pl.when(my_head + distance < head_devices)
        def _():
            greet(barrier, head=my_head + distance)

        greeted = greeted + jnp.where(my_head >= distance, 1, 0)

    @pl.when(core == 0)
    def _():
        for index in (1, 3, 0, 2):
            loads[index].start()

    @pl.when(core == 1)
    def _():
        for index in (0, 2, 1, 3):
            loads[index].start()

    row_id = lax.broadcasted_iota(jnp.int32, (rows, rows), 0)
    col_id = lax.broadcasted_iota(jnp.int32, (rows, rows), 1)
    upto_ref[...] = (row_id <= col_id).astype(F32).astype(BF16)
    stack_ref[...] = jnp.zeros_like(stack_ref)
    rows_ref[...] = jnp.zeros_like(rows_ref)

    def stacked(tensor):
        for index, piece in enumerate(thirds(tensor)):
            stack_ref[index * pad:index * pad + heads] = piece
        return stack_ref[...].astype(BF16)

    def unstacked(tensor):
        return (tensor[0:heads] + tensor[pad:pad + heads]) + tensor[2 * pad:2 * pad + heads]

    for copy in small:
        copy.wait()
    gate_rows = dot(weight_ref[...], latent_ref[...], (1, 0))
    eye = lax.broadcasted_iota(jnp.int32, (heads, heads), 0) == lax.broadcasted_iota(
        jnp.int32, (heads, heads), 1
    )
    bias = jnp.sum(jnp.where(eye, bias_ref[...], 0.0), axis=1, keepdims=True)
    gate_rows = gate_rows + bias
    log_decay = (jnp.minimum(gate_rows, 0.0) - jnp.log1p(jnp.exp(-jnp.abs(gate_rows)))) / 16.0
    cumul = unstacked(dot(stacked(log_decay), upto_ref[...], (1, 0)))
    first_pos = me * rows
    bounds = bounds_ref[...]
    position = first_pos + lax.broadcasted_iota(jnp.int32, (rows, bounds.shape[1]), 0)
    opened = jnp.where((bounds >= first_pos) & (bounds <= position), 1.0, 0.0).astype(BF16)
    docs = dot(jnp.ones((8, bounds.shape[1]), BF16), opened, (1, 1))
    doc_row = docs[0:1]
    doc_last = doc_row[:, rows - 1:]
    ending = cumul[:, rows - 1:]
    through = jnp.where(doc_last == 0.0, jnp.exp(ending), 0.0)
    rows_ref[0:heads] = jnp.where(doc_row == doc_last, jnp.exp(ending - cumul), 0.0)
    rows_ref[heads:2 * heads] = jnp.where(doc_row == 0.0, jnp.exp(cumul), 0.0) * scaling
    rows_ref[2 * heads:3 * heads] = cumul
    rows_ref[3 * heads:3 * heads + 8] = docs
    through_ref[2 * pad:2 * pad + heads] = (1.0 / (1.0 + jnp.exp(gate_rows))) / 16.0
    t_ref[place, 0:heads] = jnp.broadcast_to(through, (heads, LANES))

    def column(index):
        return cols_ref[:, index:index + 1]

    def head_lanes(index):
        return pl.ds(index * HEAD_DIM, HEAD_DIM)

    def remote(source, target, send_sem, recv_sem, **where):
        return pltpu.make_async_remote_copy(
            src_ref=source, dst_ref=target, send_sem=send_sem, recv_sem=recv_sem,
            device_id=where, device_id_type=MESH,
        )

    pl.semaphore_wait(barrier, greeted)
    for distance in range(1, blocks):

        @pl.when(block >= distance)
        def _():
            greet(block_ready.at[distance - 1], seq=me - distance * layer)

    for distance in range(1, head_devices):

        @pl.when(my_head >= distance)
        def _():
            greet(head_ready.at[distance - 1], head=my_head - distance)


    def decay_copy(target, slot):
        return remote(
            t_ref.at[slot], t_ref.at[slot], t_send,
            t_recv.at[0 if target is mate else 1], seq=target,
        )

    decay_copy(mate, place).start()

    def mate_copy(head):
        return remote(
            part_ref.at[1 - core, head], mate_in.at[head], mate_send, mate_recv.at[head], seq=mate
        )

    def span(c):
        return pl.ds(c * PIECE, PIECE)

    def block_span(c):
        return pl.ds(0, LEAD + PIECE) if c == 0 else pl.ds(LEAD + c * PIECE, PIECE)

    def rs_copy(target, source, i, c):
        return remote(
            rs_out.at[target, i, span(c)], rs_in.at[source, i, span(c)],
            rs_send, rs_recv.at[c], seq=at_chip(target),
        )

    def blk_copy(distance, i, c):
        return remote(
            blk_out.at[i, block_span(c)], blk_in.at[distance - 1, i, block_span(c)],
            blk_send.at[distance - 1], blk_recv.at[distance - 1, c], seq=at_block(distance),
        )

    def ag_copy(target, source, i, c):
        return remote(
            ag_out.at[target, i, span(c)], state_ref.at[core, source * quarter + i, span(c)],
            ag_send, ag_recv.at[source], seq=at_chip(target),
        )

    def back_copy(head):
        return remote(
            back_out.at[head], state_ref.at[core, head], back_send, back_recv, seq=mate
        )

    order = [(whose, i) for whose in (*others, chip) for i in range(quarter)]

    def part(way, head):
        lanes = pl.ds(pl.multiple_of(head * HEAD_DIM, HEAD_DIM), HEAD_DIM)
        turned = x_ref[way, :, lanes].T
        left_ref[way, head] = turned
        upper, lower = halves(turned.astype(F32) * rows_ref[pl.ds(way * heads + head, 1)])
        right = x_ref[2 + way, :, lanes]
        part_ref[way, head] = dot(upper, right, (1, 0)) + dot(lower, right, (1, 0))

    def load_wait(way):
        for index in (way, 2 + way):
            pltpu.make_async_copy(k_hbm, x_ref.at[index], load_sem.at[index]).wait()

    load_wait(1 - core)
    for first in range(0, heads, 4):
        batch = [whose * quarter + i for whose, i in order[first:first + 4]]
        for head in batch:
            part(1 - core, head)
        for head in batch:
            mate_copy(head).start()
    for whose in others:
        for peer in range(PAIR):
            decay_copy(group + whose * PAIR + peer, place).start()
    load_wait(core)
    for whose, i in order:
        part(core, whose * quarter + i)

    decay_copy(mate, place).wait_recv()

    def decay_of(index, head):
        return t_ref[index, pl.ds(head, 1), :]

    def send_parts():
        for whose, i in order:
            head = whose * quarter + i
            keep = decay_of(PAIR * chip + 1 - core, head)
            mate_copy(head).wait_recv()
            total = keep * part_ref[core, head] + mate_in[head]
            if whose is chip:
                rs_in[chip, i] = total
            else:
                rs_out[whose, i] = total
                for c in range(CHUNKS // 2):
                    rs_copy(whose, chip, i, c).start()
        for whose, i in order:
            if whose is not chip:
                for c in range(CHUNKS // 2, CHUNKS):
                    rs_copy(whose, chip, i, c).start()

    lane_id = lax.broadcasted_iota(jnp.int32, (rows, LANES), 1)

    def local_head(head):
        lanes = head_lanes(head)
        key, query, value, grad = (x_ref[index, :, lanes] for index in range(4))
        same_doc = (row_id >= col_id) & (column(3 * heads) == rows_ref[3 * heads:3 * heads + 1])
        spread = jnp.where(
            same_doc, column(2 * heads + head) - rows_ref[2 * heads + head:2 * heads + head + 1], 0.0
        )
        weights = jnp.where(same_doc, jnp.exp(spread), 0.0)
        scores = dot(query, key, (1, 1)) * scaling * weights
        pair_dots = dot(grad, value, (1, 1))
        weighted = (pair_dots * weights * scaling).astype(BF16)
        products = scores * pair_dots
        iv_ref[:, lanes] = dot(scores.astype(BF16), grad, (0, 0))
        iq_ref[:, lanes] = dot(weighted, key, (1, 0))
        ik_ref[:, lanes] = dot(weighted, query, (0, 0))
        flows.append(jnp.sum(products, axis=1, keepdims=True))
        base_ref[head:head + 1] = jnp.sum(products, axis=0, keepdims=True)

    passes_on = sends_to(1)
    pl.when(passes_on)(send_parts)
    for index in range(LANES // rank):
        tiled_ref[index * rank:(index + 1) * rank] = latent_ref[...]
    cols_ref[...] = rows_ref[...].T
    flows = []
    for head in range(heads):
        local_head(head)
    pl.when(jnp.logical_not(passes_on))(send_parts)
    gathered = jnp.zeros((rows, LANES), F32)
    for head in range(heads):
        gathered = jnp.where(lane_id == head, flows[head], gathered)
        value_ref[head] = x_ref[2, :, head_lanes(head)].T
    base_ref[0:heads] = gathered.T[0:heads] - base_ref[0:heads]

    def kth(k):
        return jnp.where(core == 0, k, CHIPS - 1 - k)

    def is_needed(target):
        begins = jnp.where(core == 0, block == 0, block == blocks - 1)
        return jnp.logical_not(begins & (target == kth(0)))

    def chip_decay(index, head):
        return decay_of(PAIR * index, head) * decay_of(PAIR * index + 1, head)

    passed = t_ref.at[pl.ds(0, layer - PAIR)]
    remote(passed, passed, t_send, t_recv.at[1], seq=mate).wait_recv()
    for distance in range(1, blocks):

        @pl.when(block + distance < blocks)
        def _():
            pl.semaphore_wait(block_ready.at[distance - 1], 1)

    for c in range(CHUNKS):
        passed = rs_in.at[pl.ds(0, CHIPS - 1), :, span(c)]
        remote(passed, passed, rs_send, rs_recv.at[c], seq=mate).wait_recv()
        for i in range(quarter):
            head = chip * quarter + i
            total = rs_in[kth(0), i, span(c)]
            for k in range(1, CHIPS):
                total = chip_decay(kth(k), head) * total + rs_in[kth(k), i, span(c)]
            blk_out[i, pl.ds(LEAD + c * PIECE, PIECE)] = total
            if c == 0:
                across = chip_decay(0, head)
                for k in range(1, CHIPS):
                    across = across * chip_decay(k, head)
                blk_out[i, 0:LEAD] = jnp.broadcast_to(across, (LEAD, LANES))
            for distance in range(1, blocks):
                pl.when(sends_to(distance))(blk_copy(distance, i, c).start)

    for c in range(CHUNKS):
        for i in range(quarter):
            entering = jnp.zeros((PIECE, HEAD_DIM), F32)
            for distance in range(blocks - 1, 0, -1):
                hears = hears_from(distance)
                pl.when(hears)(blk_copy(distance, i, c).wait_recv)

                @pl.when(jnp.logical_not(hears))
                def _():
                    blk_in[distance - 1, i, block_span(c)] = jnp.zeros(
                        (PIECE + (LEAD if c == 0 else 0), HEAD_DIM), F32
                    )

                entering = (
                    blk_in[distance - 1, i, 0:1] * entering
                    + blk_in[distance - 1, i, pl.ds(LEAD + c * PIECE, PIECE)]
                )
            head = chip * quarter + i
            for k in range(CHIPS):
                ag_out[kth(k), i, span(c)] = entering
                if k < CHIPS - 1:
                    entering = chip_decay(kth(k), head) * entering + rs_in[kth(k), i, span(c)]
            for target in others:
                pl.when(is_needed(target))(ag_copy(target, chip, i, c).start)

    for whose in (chip, beside, above, opposite):
        mine = pl.ds(whose * quarter, quarter)
        if whose is not chip:
            arriving = remote(
                ag_out.at[whose], state_ref.at[core, mine], ag_send, ag_recv.at[whose], seq=mate
            )
            pl.when(is_needed(chip))(arriving.wait_recv)

            @pl.when(jnp.logical_not(is_needed(chip)))
            def _():
                state_ref[core, mine] = jnp.zeros((quarter, HEAD_DIM, HEAD_DIM), F32)

        for i in range(quarter):
            head = whose * quarter + i
            if whose is chip:
                state_ref[core, head] = ag_out[chip, i]
            back_out[head] = decay_of(place, head) * state_ref[core, head] + part_ref[core, head]
            back_copy(head).start()

    def state_rows():
        for head in range(heads):
            upper, lower = halves(state_ref[0, head])
            grad = x_ref[3, :, head_lanes(head)]
            carried = dot(upper, grad, (1, 1)) + dot(lower, grad, (1, 1))
            inflow = jnp.sum(carried * left_ref[1, head].astype(F32), axis=0, keepdims=True)
            through_ref[head:head + 1] = inflow * rows_ref[heads + head:heads + head + 1]

    def back_rows():
        for head in range(heads):
            upper, lower = halves(state_ref[1, head])
            key = x_ref[0, :, head_lanes(head)]
            carried = dot(upper, key, (0, 1)) + dot(lower, key, (0, 1))
            outflow = jnp.sum(carried * value_ref[head].astype(F32), axis=0, keepdims=True)
            through_ref[pad + head:pad + head + 1] = outflow * rows_ref[head:head + 1]

    def finish_heads():
        for head in range(heads):
            lanes = head_lanes(head)
            key, query, value, grad = (x_ref[index, :, lanes] for index in range(4))
            enter, leave = column(heads + head), column(head)
            upper, lower = halves(state_ref[0, head])
            carried = (dot(grad, upper, (1, 1)) + dot(grad, lower, (1, 1))) * enter
            gq_ref[:, lanes] = (iq_ref[:, lanes] + carried).astype(BF16)
            upper, lower = halves(state_ref[1, head])
            carried = (dot(key, upper, (1, 0)) + dot(key, lower, (1, 0))) * leave
            gv_ref[:, lanes] = (iv_ref[:, lanes] + carried).astype(BF16)
            carried = dot(value, upper, (1, 1)) * leave
            gk_ref[:, lanes] = (ik_ref[:, lanes] + carried).astype(BF16)

    pl.when(core == 0)(state_rows)
    pl.when(core == 1)(back_rows)
    remote(back_out, state_ref.at[1 - core], back_send, back_recv, seq=mate).wait_recv()
    pl.when(core == 0)(back_rows)
    pl.when(core == 1)(state_rows)

    wholes = [
        jnp.sum(jnp.sum(state_ref[0, head] * state_ref[1, head], axis=0, keepdims=True), axis=1, keepdims=True)
        for head in range(heads)
    ]
    inflow, outflow = through_ref[0:heads], through_ref[pad:pad + heads]
    end_term = through * jnp.concatenate(wholes, axis=0) + jnp.sum(outflow, axis=1, keepdims=True)
    row_lane = lax.broadcasted_iota(jnp.int32, (heads, rows), 1)
    grad_cumul = base_ref[0:heads] + (inflow - outflow) + jnp.where(
        row_lane == rows - 1, end_term, 0.0
    )
    grad_log = unstacked(dot(stacked(grad_cumul), upto_ref[...], (1, 1)))
    grad_gate = grad_log * through_ref[2 * pad:2 * pad + heads]
    pieces = stacked(grad_gate)
    spread = unstacked(dot(pieces, tiled_ref[...], (1, 1)))
    lane = lax.broadcasted_iota(jnp.int32, (heads, LANES), 1)
    owner = lax.broadcasted_iota(jnp.int32, (heads, LANES), 0)
    gw_slots[flat] = jnp.sum(
        jnp.where(lax.div(lane, rank) == owner, spread, 0.0), axis=0, keepdims=True
    )
    for away in range(1, members):
        remote(
            gw_slots.at[flat], gw_slots.at[flat], gw_send, gw_recv,
            **member(lax.rem(flat + away, members)),
        ).start()
    weight = weight_ref[...]
    lat_slots[my_head] = (
        dot(weight, pieces[0:heads], (0, 0)) + dot(weight, pieces[pad:pad + heads], (0, 0))
    ) + dot(weight, pieces[2 * pad:2 * pad + heads], (0, 0))

    for distance in range(1, head_devices):

        @pl.when(my_head + distance < head_devices)
        def _():
            pl.semaphore_wait(head_ready.at[distance - 1], 1)

    for away in range(1, head_devices):
        remote(
            lat_slots.at[my_head], lat_slots.at[my_head], lat_send, lat_recv,
            head=lax.rem(my_head + away, head_devices),
        ).start()

    finish_heads()
    passed = t_ref.at[pl.ds(0, layer - 1)]
    remote(passed, passed, t_send, t_recv.at[0], seq=mate).wait_send()
    remote(mate_in, mate_in, mate_send, mate_recv.at[0], seq=mate).wait_send()
    passed = rs_out.at[pl.ds(0, CHIPS - 1)]
    remote(passed, passed, rs_send, rs_recv.at[0], seq=mate).wait_send()
    for target in others:
        pl.when(is_needed(target))(
            remote(
                ag_out.at[target], ag_out.at[target], ag_send, ag_recv.at[0], seq=mate
            ).wait_send
        )
    remote(back_out, back_out, back_send, back_recv, seq=mate).wait_send()
    for distance in range(1, blocks):
        pl.when(sends_to(distance))(
            remote(
                blk_out, blk_out, blk_send.at[distance - 1], blk_recv.at[0, 0], seq=mate
            ).wait_send
        )
    peer = {"head": lax.rem(my_head + 1, head_devices)}
    if head_devices > 1:
        passed = lat_slots.at[pl.ds(0, head_devices - 1)]
        lats = remote(passed, passed, lat_send, lat_recv, **peer)
        lats.wait_recv()
    total = lat_slots[0]
    for slot in range(1, head_devices):
        total = total + lat_slots[slot]
    glat_ref[...] = total
    passed = gw_slots.at[pl.ds(0, members - 1)]
    sums = remote(passed, passed, gw_send, gw_recv, seq=mate)
    sums.wait_recv()
    total = gw_slots[0]
    for slot in range(1, members):
        total = total + gw_slots[slot]
    gw_ref[...] = total

    if head_devices > 1:
        lats.wait_send()
    sums.wait_send()


def emit_kernel(gq, gk, gv, glat, gw, oq, ok, ov, olat, ow):
    oq[...] = gq[...]
    ok[...] = gk[...]
    ov[...] = gv[...]
    olat[...] = glat[...]
    for head in range(ow.shape[0]):
        ow[head:head + 1] = gw[:, head * ow.shape[1]:(head + 1) * ow.shape[1]]


def emit(results, rows, width, rank, heads):
    vmem = pl.BlockSpec(memory_space=pltpu.VMEM)
    hbm = pl.BlockSpec(memory_space=pl.ANY)
    wide = jax.ShapeDtypeStruct((rows, width), BF16)
    return pl.pallas_call(
        emit_kernel,
        out_shape=(
            wide, wide, wide,
            jax.ShapeDtypeStruct((rank, rows), F32), jax.ShapeDtypeStruct((heads, rank), F32),
        ),
        in_specs=[vmem] * 5,
        out_specs=(vmem,) * 5,

        name="emit",
    )(*(pltpu.with_memory_space_constraint(result, pltpu.VMEM) for result in results))


def on_device(sizes, *args):
    queries, keys_in, values, grad_out, latent, gate_weight, gate_bias, doc_starts, block_docs = args
    rows, width = queries.shape[1], queries.shape[2]
    rank = latent.shape[2]
    seq_count, dp_count, head_devices = sizes
    heads = width // HEAD_DIM
    quarter = heads // CHIPS
    layer = PAIR * CHIPS
    far = max(1, seq_count // layer - 1)
    members = seq_count * dp_count
    pad = -(-heads // 8) * 8
    square = lambda *lead: pltpu.VMEM((*lead, HEAD_DIM, HEAD_DIM), F32)
    dma = lambda *shape: pltpu.SemaphoreType.DMA(shape)
    single = pltpu.SemaphoreType.DMA
    hbm = pl.BlockSpec(memory_space=pltpu.HBM)
    wide = pltpu.VMEM((rows, width), BF16)
    results = pl.pallas_call(
        functools.partial(kernel, (seq_count, dp_count, head_devices, heads)),
        out_shape=(
            wide, wide, wide, pltpu.VMEM((rank, rows), F32), pltpu.VMEM((1, LANES), F32),
        ),
        in_specs=[hbm] * 8,
        scratch_shapes=[
            pltpu.VMEM((4, rows, width), BF16),
            pltpu.VMEM((rank, rows), BF16),
            pltpu.VMEM((heads, rank), BF16),
            pltpu.VMEM((1, heads), F32),
            pltpu.VMEM(doc_starts.shape, jnp.int32),
            pltpu.VMEM((LANES, rows), BF16),
            pltpu.VMEM((3 * pad, rows), F32),
            pltpu.VMEM((LANES, rows), F32),
            pltpu.VMEM((rows, LANES), F32),
            pltpu.VMEM((rows, rows), BF16),
            pltpu.VMEM((rows, width), F32),
            pltpu.VMEM((rows, width), F32),
            pltpu.VMEM((rows, width), F32),
            pltpu.VMEM((2, heads, HEAD_DIM, rows), BF16),
            pltpu.VMEM((heads, HEAD_DIM, rows), BF16),
            pltpu.VMEM((pad, rows), F32),
            pltpu.VMEM((3 * pad, rows), F32),
            pltpu.VMEM((layer, 8, LANES), F32),
            square(2, heads), square(heads), square(CHIPS, quarter), square(CHIPS, quarter),
            pltpu.VMEM((quarter, LEAD + HEAD_DIM, HEAD_DIM), F32),
            pltpu.VMEM((far, quarter, LEAD + HEAD_DIM, HEAD_DIM), F32),
            square(CHIPS, quarter), square(heads), square(2, heads),
            pltpu.VMEM((head_devices, rank, rows), F32),
            pltpu.VMEM((members, 1, LANES), F32),
            dma(4), dma(4), single, dma(2), single, dma(heads), single, dma(CHUNKS),
            dma(far), dma(far, CHUNKS), single, dma(CHIPS), single, single,
            single, single, single, single,
            pltpu.SemaphoreType.REGULAR((far,)),
            pltpu.SemaphoreType.REGULAR((max(1, head_devices - 1),)),
        ],
        compiler_params=pltpu.CompilerParams(collective_id=0, has_side_effects=True),
        name="gated_backward",
    )(
        keys_in[0], queries[0], values[0], grad_out[0], latent[0].T, gate_weight.T,
        gate_bias[None, :], doc_starts,
    )
    out = emit(results, rows, width, rank, heads)
    return out[0][None], out[1][None], out[2][None], out[3].T[None], out[4].T


def solution(mesh):
    sizes = (mesh.shape["seq"], mesh.shape["dp"], mesh.shape["head"])
    return jax.shard_map(
        functools.partial(on_device, sizes),
        mesh=mesh,
        in_specs=(
            P(("groups", "dp"), "seq", "head"),
            P(("groups", "dp"), "seq", "head"),
            P(("groups", "dp"), "seq", "head"),
            P(("groups", "dp"), "seq", "head"),
            P(("groups", "dp"), "seq", None),
            P(None, "head"),
            P("head"),
            P(("groups", "dp"), None),
            P(("groups", "dp"), "seq"),
        ),
        out_specs=(
            P(("groups", "dp"), "seq", "head"),
            P(("groups", "dp"), "seq", "head"),
            P(("groups", "dp"), "seq", "head"),
            P(("groups", "dp"), "seq", None),
            P("groups", "head"),
        ),
        check_vma=False,
    )
```
